32 devices in a mesh: wave: 4 (over z), tile: 8 (over y, x, core).
Axes of the slice: x: 2, y: 2, z: 4, core: 2. Of those that a mesh axis runs over, the one named last changes fastest.
Arguments:
- initial_fields: bfloat16 [16, 8, 256, 1024], P('wave', None, 'tile'), may hold values from -6 to 6
- conductivity: float32 [256, 1024], P('tile'), may hold values from 0.1 to 10
- wavenumbers: float32 [16], replicated, may hold values from 0.05 to 1.5
- quad_weights: float32 [16], replicated, may hold values from 0.05 to 0.3
- sweep_counts: int32 [16], replicated, may hold values from 1 to 8, as said below
- electrode_cells: int32 [64], replicated, may hold values from 0 to 255
- source_pairs: int32 [8, 2], replicated, may hold values from 0 to 63, as said below
Outputs:
- potential: float32 [8, 256, 1024], P('wave', 'tile')
The draws below stay inside these ranges and needn't reach their ends.
Inputs may be any that keep to these rules, and one draw needn't show every extreme that they name: `sweep_counts`: each wavenumber gets at least one sweep and at most 8. `source_pairs`: the two electrodes of a source column are different electrodes.
All inputs are finite; a program needn't handle non-finite values.
Results may differ from the reference program's by a relative error of at most 0.0003.
Values may be sent and summed in bfloat16 or wider, within the bound.
No kernel may reach another device: no remote copies, remote signals or barrier semaphores. Data moves between devices by JAX's collectives and lax.ppermute only.
A program may use at most 64 MiB of HBM per device.

```python
import math
import jax
import jax.numpy as jnp
from jax import lax

NY = 1024
SRC = 8
KD = 4
ITERS = 8
ELEC = 64
KNUM = 16
NX = 256


def draw_sweep_counts(key, part):
    keys = jax.random.split(key, 4)
    groups = KNUM // KD
    index = jnp.arange(KNUM, dtype=jnp.int32)
    heavy = jax.random.randint(keys[0], (), 0, groups)
    high = jax.random.randint(keys[1], (KNUM,), ITERS // 2 + 2, ITERS + 1)
    low = jax.random.randint(keys[2], (KNUM,), 1, ITERS // 2)
    counts = jnp.where(index // KD == heavy, high, low)
    top = heavy * KD + jax.random.randint(keys[3], (), 0, KD)
    bottom = (heavy + 1) % groups * KD
    counts = jnp.where(index == top, ITERS, counts)
    counts = jnp.where(index == bottom, 1, counts)
    return counts.astype(jnp.int32)


def draw_source_pairs(key, part):
    keys = jax.random.split(key, 2)
    first = jax.random.randint(keys[0], (SRC,), 0, ELEC)
    offset = jax.random.randint(keys[1], (SRC,), 1, ELEC)
    second = (first + offset) % ELEC
    return jnp.stack([first, second], axis=1).astype(jnp.int32)


def set_ends(values, stream_key, smallest, high):
    place = [jax.random.randint(jax.random.fold_in(stream_key, axis), (), 0, length) for axis, length in enumerate(values.shape)]
    main_axis = values.shape.index(max(values.shape))
    next_to = place[:main_axis] + [(place[main_axis] + 1) % values.shape[main_axis]] + place[main_axis + 1:]
    return values.at[tuple(place)].set(smallest).at[tuple(next_to)].set(high)


def steps_of(stream_key, extent, pieces, low, high):
    def one(axis_at, shards_of):
        steps = jax.random.uniform(jax.random.fold_in(jax.random.fold_in(stream_key, 6), axis_at), (shards_of,), jnp.float32, low / len(pieces), high / len(pieces))
        return jnp.repeat(jnp.exp(steps), extent[axis_at] // shards_of).reshape((-1,) + (1,) * (len(extent) - axis_at - 1))

    level = one(*pieces[0])
    for cut in pieces[1:]:
        level = level * one(*cut)
    return level


def noise(rng, shape, spread, most, cuts=(), held_as=jnp.bfloat16):
    result = jax.random.normal(rng, shape, jnp.float32) * spread
    if len(cuts) > 0:
        result = steps_of(rng, shape, cuts, -0.22, 0.18) * result
    return jnp.clip(result, min=-most, max=most).astype(held_as)


def setup_inputs(seed: int = 0) -> dict:
    arg_keys = jax.random.split(jax.random.key(seed), 8)
    return {
        "initial_fields": noise(arg_keys[0], (KNUM, SRC, NX, NY), 1.0, 6.0, ((0, 4), (2, 8))),
        "conductivity": jnp.clip(jnp.exp(math.log(10.0) - 4.6051702 * jax.random.uniform(arg_keys[1], (NX, NY), jnp.float32) ** steps_of(arg_keys[1], (NX, NY), ((0, 8),), -0.2, 0.2)), 0.1, 10.0),
        "wavenumbers": jnp.clip(jnp.exp(jax.random.uniform(arg_keys[2], (KNUM,), jnp.float32, math.log(0.05), math.log(1.5))), 0.05, 1.5),
        "quad_weights": jnp.clip(jnp.exp(jax.random.uniform(arg_keys[3], (KNUM,), jnp.float32, math.log(0.05), math.log(0.3))), 0.05, 0.3),
        "sweep_counts": draw_sweep_counts(jax.random.fold_in(arg_keys[7], 71), 0),
        "electrode_cells": set_ends(jax.random.randint(arg_keys[5], (ELEC,), 0, NX), jax.random.fold_in(arg_keys[5], 1), 0, NX - 1).astype(jnp.int32),
        "source_pairs": draw_source_pairs(jax.random.fold_in(arg_keys[7], 71), 0),
    }


LOWER = 0.1
UPPER = 2.0
THETA = (UPPER + LOWER) / 2.0
DELTA = (UPPER - LOWER) / 2.0
SIGMA_ONE = THETA / DELTA
CURRENT = 2.0


def face_values(conductivity):
    padded = jnp.pad(conductivity, 1)
    face_north = 0.5 * (conductivity + padded[:-2, 1:-1])
    face_south = 0.5 * (conductivity + padded[2:, 1:-1])
    face_west = 0.5 * (conductivity + padded[1:-1, :-2])
    face_east = 0.5 * (conductivity + padded[1:-1, 2:])
    return face_north, face_south, face_west, face_east


def neighbours(padded_rows, facets):
    face_north, face_south, face_west, face_east = facets
    centre = padded_rows[:, 1:-1]
    columns = jnp.pad(centre, ((0, 0), (0, 0), (1, 1)))
    total = face_north * padded_rows[:, :-2] + face_south * padded_rows[:, 2:]
    return total + face_west * columns[:, :, :-2] + face_east * columns[:, :, 2:]


def chebyshev_step(step, field, direction, rho_prev, residual, diag_k, active):
    scaled = residual / diag_k
    rho_next = 1.0 / (2.0 * SIGMA_ONE - rho_prev)
    first = step == 0
    keep = jnp.where(first, 0.0, rho_next * rho_prev)
    gain = jnp.where(first, 1.0 / THETA, 2.0 * rho_next / DELTA)
    moved = keep * direction + gain * scaled
    new_rho = jnp.where(first, 1.0 / SIGMA_ONE, rho_next)
    return (jnp.where(active, field + moved, field), jnp.where(active, moved, direction), jnp.where(active, new_rho, rho_prev))


def reference(initial_fields, conductivity, wavenumbers, quad_weights, sweep_counts, electrode_cells, source_pairs):
    facets = face_values(conductivity)
    diagonal = facets[0] + facets[1] + facets[2] + facets[3]
    row_ids = jnp.arange(NX, dtype=jnp.int32)
    column_one = (jnp.arange(NY, dtype=jnp.int32) == 0).astype(jnp.float32)
    electrode_rows = electrode_cells[source_pairs]
    positive = (row_ids[None, :] == electrode_rows[:, 0:1]).astype(jnp.float32)
    negative = (row_ids[None, :] == electrode_rows[:, 1:2]).astype(jnp.float32)
    sources = CURRENT * (positive - negative)[:, :, None] * column_one[None, None, :]

    def per_wave(summed, item):
        field_start, wavenumber, weight, count = item
        diag_k = diagonal + wavenumber * wavenumber * conductivity

        def sweep(step, carry):
            field_now, dir_now, rho_now = carry
            padded = jnp.pad(field_now, ((0, 0), (1, 1), (0, 0)))
            residual = sources - (diag_k * field_now - neighbours(padded, facets))
            return chebyshev_step(step, field_now, dir_now, rho_now, residual, diag_k, True)

        start = field_start.astype(jnp.float32)
        rho_start = jnp.full((start.shape[0], 1, 1), 1.0 / SIGMA_ONE, jnp.float32)
        solved = lax.fori_loop(0, count, sweep, (start, jnp.zeros_like(start), rho_start))[0]
        return summed + weight * solved, None

    summed, _ = lax.scan(per_wave, jnp.zeros((SRC, NX, NY), jnp.float32), (initial_fields, wavenumbers, quad_weights, sweep_counts))
    return summed
```

```python
import functools

import jax
import jax.numpy as jnp
from jax import lax
from jax.experimental import pallas as pl
from jax.experimental.pallas import tpu as pltpu
from jax.sharding import PartitionSpec as P

ITERS = 8
LOWER = 0.1
UPPER = 2.0
THETA = (UPPER + LOWER) / 2.0
DELTA = (UPPER - LOWER) / 2.0
SIGMA_ONE = THETA / DELTA
CURRENT = 2.0
DIAG = 2.0 * (THETA - 1.0) / DELTA
LANES = 128
SUB = 8


def chebyshev_table():
    values = [1.0, SIGMA_ONE]
    for _ in range(ITERS):
        values.append(2.0 * SIGMA_ONE * values[-1] - values[-2])
    return values


TABLE = chebyshev_table()


def coefficients_kernel(squares, cond_lo, cond, cond_hi, c_north, c_east, root, q_first, cond_pad, q_pad):
    rows, cols = cond.shape
    halo = cond_lo.shape[0]
    tall = rows + 2 * halo
    waves = root.shape[0]
    pair = SUB // waves
    cond_pad[pl.ds(0, halo), :] = jnp.zeros((halo, cols), jnp.float32)
    cond_pad[pl.ds(halo, halo), :] = cond_lo[...]
    cond_pad[pl.ds(2 * halo, rows), :] = cond[...]
    cond_pad[pl.ds(2 * halo + rows, halo), :] = cond_hi[...]
    cond_pad[pl.ds(3 * halo + rows, halo), :] = jnp.zeros((halo, cols), jnp.float32)
    lane = lax.broadcasted_iota(jnp.int32, (SUB, cols), 1)

    def faces(base):
        mid = cond_pad[pl.ds(base, SUB), :]
        up = cond_pad[pl.ds(base - 1, SUB), :]
        down = cond_pad[pl.ds(base + 1, SUB), :]
        east = 0.5 * (mid + jnp.where(lane == cols - 1, 0.0, pltpu.roll(mid, cols - 1, 1)))
        west = 0.5 * (mid + jnp.where(lane == 0, 0.0, pltpu.roll(mid, 1, 1)))
        return mid, 0.5 * (mid + up), 0.5 * (mid + down), east, west

    q_pad[...] = jnp.zeros(q_pad.shape, jnp.float32)
    for tile in range(tall // SUB):
        base = tile * SUB
        mid, north, south, east, west = faces(halo + base)
        diagonal = north + south + west + east
        inside = mid > 0.0
        for w in range(waves):
            sq = jnp.sqrt(diagonal + squares[w] * mid)
            root[w, pl.ds(base, SUB), :] = sq
            q_pad[w, pl.ds(halo + base, SUB), :] = jnp.where(inside, 1.0 / sq, 0.0)
    for tile in range(tall // SUB):
        base = tile * SUB
        mid, north, south, east, west = faces(halo + base)
        inside = mid > 0.0
        edge = jnp.where(lane == cols - 1, 0.0, east)
        for w in range(waves):
            q = q_pad[w, pl.ds(halo + base, SUB), :]
            q_up = q_pad[w, pl.ds(halo + base - 1, SUB), :]
            scaled = (2.0 / DELTA) * q
            north_w = scaled * q_up * north
            east_w = scaled * pltpu.roll(q, cols - 1, 1) * edge
            for s in range(pair):
                spot = pl.ds(base * SUB + w * pair + s, SUB, stride=SUB)
                q_first[spot, :] = jnp.where(lane[:, :LANES] == 0, q[:, :LANES], 0.0)
                for j in range(cols // LANES):
                    c_north[j, spot, :] = north_w[:, j * LANES:(j + 1) * LANES]
                    c_east[j, spot, :] = east_w[:, j * LANES:(j + 1) * LANES]


def sweep_kernel(
    counts, levels, scale, electrodes, first_row,
    lo, own, hi, c_north, c_east, root, q_first, out, u_even, u_odd,
):
    waves, sources, rows, cols = own.shape
    halo = lo.shape[2]
    pair = SUB // waves
    chunks = sources // pair
    tall = rows + 2 * halo
    limit = levels[0]
    ids = lax.broadcasted_iota(jnp.int32, (SUB, LANES), 0)
    lanes = lax.broadcasted_iota(jnp.int32, (SUB, LANES), 1)

    width = cols // LANES

    def rows_of(ref, r):
        spot = pl.ds(pl.multiple_of(r * SUB, SUB), SUB)
        return tuple(ref[j, spot, :] for j in range(width))

    def one_chunk(c, _):
        for w in range(waves):
            for s in range(pair):
                i = w * pair + s
                for ref, start in ((lo, 0), (own, halo), (hi, halo + rows)):
                    for tile in range(ref.shape[2] // SUB):
                        base = start + tile * SUB
                        part = ref[w, c * pair + s, pl.ds(tile * SUB, SUB), :].astype(jnp.float32)
                        part = part * root[w, pl.ds(base, SUB), :]
                        for j in range(width):
                            u_even[j, pl.ds(base * SUB + i, SUB, stride=SUB), :] = (
                                part[:, j * LANES:(j + 1) * LANES]
                            )
        out[pl.ds(c * pair, pair)] = jnp.zeros((pair, rows, cols), jnp.float32)

        def level(t, src, dst, first):
            depth = limit - t
            begin = halo - depth
            boost = scale[t]

            def row(r, up, mid, north):
                down = rows_of(src, r + 1)
                south = rows_of(c_north, r + 1)
                east = rows_of(c_east, r)
                spot = pl.ds(pl.multiple_of(r * SUB, SUB), SUB)
                left = [pltpu.roll(v, LANES - 1, 1) for v in mid]
                right = [pltpu.roll(e * v, 1, 1) for e, v in zip(east, mid)]
                for j in range(width):
                    from_east = left[j] if j == width - 1 else jnp.where(lanes == LANES - 1, left[j + 1], left[j])
                    from_west = jnp.where(lanes == 0, right[j - 1], right[j])
                    total = (
                        (north[j] * up[j] + south[j] * down[j])
                        + (east[j] * from_east + from_west) + DIAG * mid[j]
                    )
                    if first:
                        total = 0.5 * total
                    else:
                        total = total - dst[j, spot, :]
                    dst[j, spot, :] = total
                return mid, down, south

            def body(k, carry):
                r = begin + 2 * k
                carry = row(r, *carry)
                return row(r + 1, *carry)

            lax.fori_loop(
                0, rows // 2 + depth, body,
                (rows_of(src, begin - 1), rows_of(src, begin), rows_of(c_north, begin)),
            )

            for s in range(pair):
                for pole, sign in ((0, 1.0), (1, -1.0)):
                    r = electrodes[(c * pair + s) * 2 + pole] - first_row[0] + halo

                    @pl.when(jnp.logical_and(r >= begin, r < begin + rows + 2 * depth))
                    def _():
                        spot = pl.ds(pl.multiple_of(r * SUB, SUB), SUB)
                        add = jnp.where(lax.rem(ids, pair) == s, q_first[spot, :], 0.0)
                        dst[0, spot, :] = dst[0, spot, :] + (sign * boost) * add

            for w in range(waves):

                @pl.when(counts[w] == t)
                def _():
                    for tile in range(rows // SUB):
                        base = halo + tile * SUB
                        factor = counts_scale(w, t) / root[w, pl.ds(base, SUB), :]
                        for s in range(pair):
                            spot = pl.ds(base * SUB + w * pair + s, SUB, stride=SUB)
                            for j in range(width):
                                here = (c * pair + s, pl.ds(tile * SUB, SUB), pl.ds(j * LANES, LANES))
                                part = factor[:, j * LANES:(j + 1) * LANES]
                                out[here] = out[here] + part * dst[j, spot, :]

        def counts_scale(w, t):
            return scale[ITERS + 1 + w] * scale[ITERS + 1 + waves + t]

        level(1, u_even, u_odd, True)

        def two(k, _):
            level(2 * k, u_odd, u_even, False)

            @pl.when(2 * k + 1 <= limit)
            def _():
                level(2 * k + 1, u_even, u_odd, False)

            return 0

        lax.fori_loop(1, limit // 2 + 1, two, 0)
        return 0

    lax.fori_loop(0, chunks, one_chunk, 0)


def local(
    initial_fields, conductivity, wavenumbers, quad_weights, sweep_counts, electrode_cells,
    source_pairs,
):
    row_count, col_count = conductivity.shape
    waves, sources = initial_fields.shape[:2]
    halo = ITERS
    tile_pos = lax.axis_index("tile")
    wave_pos = lax.axis_index("wave")
    count = lax.axis_size("tile")
    forward = [(i, i + 1) for i in range(count - 1)]
    backward = [(i + 1, i) for i in range(count - 1)]
    cond_lo = lax.ppermute(conductivity[-halo:], "tile", forward)
    cond_hi = lax.ppermute(conductivity[:halo], "tile", backward)
    lo = lax.ppermute(initial_fields[:, :, -halo:], "tile", forward)
    hi = lax.ppermute(initial_fields[:, :, :halo], "tile", backward)
    mine = lambda v: lax.dynamic_slice_in_dim(v, wave_pos * waves, waves)
    values, weights, counts = mine(wavenumbers), mine(quad_weights), mine(sweep_counts)
    electrodes = electrode_cells[source_pairs.reshape(-1)]
    sources_scale = [0.0, CURRENT / DELTA] + [2.0 * CURRENT / DELTA * TABLE[t] for t in range(1, ITERS)]
    ends = [0.0] + [1.0 / TABLE[t] for t in range(1, ITERS + 1)]
    scale = jnp.concatenate(
        [jnp.array(sources_scale, jnp.float32), weights, jnp.array(ends, jnp.float32)]
    )
    tall = row_count + 2 * halo
    smem = pl.BlockSpec(memory_space=pltpu.SMEM)
    vmem = pl.BlockSpec(memory_space=pltpu.VMEM)
    wide = jax.ShapeDtypeStruct((col_count // LANES, tall * SUB, LANES), jnp.float32)
    c_north, c_east, root, q_first = pl.pallas_call(
        coefficients_kernel,
        out_shape=(wide, wide, jax.ShapeDtypeStruct((waves, tall, col_count), jnp.float32),
                   jax.ShapeDtypeStruct((tall * SUB, LANES), jnp.float32)),
        in_specs=[smem, vmem, vmem, vmem],
        out_specs=[vmem] * 4,
        scratch_shapes=[
            pltpu.VMEM((tall + 2 * halo, col_count), jnp.float32),
            pltpu.VMEM((waves, tall + 2 * halo, col_count), jnp.float32),
        ],
        name="coefficients",
    )(values * values, cond_lo, conductivity, cond_hi)
    summed = pl.pallas_call(
        sweep_kernel,
        out_shape=jax.ShapeDtypeStruct((sources, row_count, col_count), jnp.float32),
        in_specs=[smem] * 5 + [vmem] * 7,
        out_specs=vmem,
        scratch_shapes=[pltpu.VMEM((col_count // LANES, tall * SUB, LANES), jnp.float32)] * 2,
        name="sweeps",
    )(
        counts, jnp.max(counts)[None], scale, electrodes, (tile_pos * row_count)[None],
        lo, initial_fields, hi, c_north, c_east, root, q_first,
    )
    parts = lax.all_to_all(summed.reshape((lax.axis_size("wave"), -1, row_count, col_count)), "wave", 0, 0)
    return jnp.sum(parts, axis=0)


def solution(mesh):
    placed = (P("wave", None, "tile", None), P("tile", None), P(), P(), P(), P(), P())
    return jax.shard_map(
        local, mesh=mesh, in_specs=placed, out_specs=P("wave", "tile", None), check_vma=False
    )
```

```python
import functools

import jax
import jax.numpy as jnp
from jax import lax
from jax.experimental import pallas as pl
from jax.experimental.pallas import tpu as pltpu
from jax.sharding import PartitionSpec as P

ITERS = 8
LOWER = 0.1
UPPER = 2.0
THETA = (UPPER + LOWER) / 2.0
DELTA = (UPPER - LOWER) / 2.0
SIGMA_ONE = THETA / DELTA
CURRENT = 2.0
DIAG = 2.0 * (THETA - 1.0) / DELTA
LANES = 128
SUB = 8
UNROLL = 4


def chebyshev_table():
    values = [1.0, SIGMA_ONE]
    for _ in range(ITERS):
        values.append(2.0 * SIGMA_ONE * values[-1] - values[-2])
    return values


TABLE = chebyshev_table()


def pick(values, t):
    result = jnp.float32(values[0])
    for k in range(1, len(values)):
        result = jnp.where(t == k, jnp.float32(values[k]), result)
    return result


def coefficients_kernel(
    wavenumbers, cond_lo, cond, cond_hi, c_north, c_east, root, inverse, q_first, cond_pad, q_pad
):
    rows, cols = cond.shape
    halo = cond_lo.shape[0]
    tall = rows + 2 * halo
    waves = root.shape[0]
    pair = SUB // waves
    first = lax.axis_index("wave") * waves
    cond_pad[pl.ds(0, halo), :] = jnp.zeros((halo, cols), jnp.float32)
    cond_pad[pl.ds(halo, halo), :] = cond_lo[...]
    cond_pad[pl.ds(2 * halo, rows), :] = cond[...]
    cond_pad[pl.ds(2 * halo + rows, halo), :] = cond_hi[...]
    cond_pad[pl.ds(3 * halo + rows, halo), :] = jnp.zeros((halo, cols), jnp.float32)
    lane = lax.broadcasted_iota(jnp.int32, (SUB, cols), 1)
    q_pad[:, pl.ds(0, halo), :] = jnp.zeros((waves, halo, cols), jnp.float32)
    for tile in range(tall // SUB):
        base = tile * SUB
        mid = cond_pad[pl.ds(halo + base, SUB), :]
        up = cond_pad[pl.ds(halo + base - 1, SUB), :]
        down = cond_pad[pl.ds(halo + base + 1, SUB), :]
        north = 0.5 * (mid + up)
        south = 0.5 * (mid + down)
        east = 0.5 * (mid + jnp.where(lane == cols - 1, 0.0, pltpu.roll(mid, cols - 1, 1)))
        west = 0.5 * (mid + jnp.where(lane == 0, 0.0, pltpu.roll(mid, 1, 1)))
        diagonal = north + south + west + east
        inside = mid > 0.0
        inner = jnp.where(lane == cols - 1, 0.0, east)
        for w in range(waves):
            k = wavenumbers[first + w]
            sq = jnp.sqrt(diagonal + (k * k) * mid)
            root[w, pl.ds(base, SUB), :] = sq
            q = jnp.where(inside, 1.0 / sq, 0.0)
            if halo <= base < halo + rows:
                inverse[w, pl.ds(base - halo, SUB), :] = q
            q_pad[w, pl.ds(halo + base, SUB), :] = q
            q_up = q_pad[w, pl.ds(halo + base - 1, SUB), :]
            scaled = (2.0 / DELTA) * q
            north_w = scaled * q_up * north
            east_w = scaled * pltpu.roll(q, cols - 1, 1) * inner
            for s in range(pair):
                spot = pl.ds(base * SUB + w * pair + s, SUB, stride=SUB)
                q_first[spot, :] = jnp.where(lane[:, :LANES] == 0, q[:, :LANES], 0.0)
                for j in range(cols // LANES):
                    c_north[j, spot, :] = north_w[:, j * LANES:(j + 1) * LANES]
                    c_east[j, spot, :] = east_w[:, j * LANES:(j + 1) * LANES]


def sweep_kernel(
    shift, counts, weights, cells, pairs,
    lo, own, hi, c_north, c_east, root, inverse, q_first, out, u_even, u_odd, inject,
):
    waves, sources, rows, cols = own.shape
    halo = lo.shape[2]
    pair = out.shape[0]
    tall = rows + 2 * halo
    width = cols // LANES
    wave_pos = lax.axis_index("wave")
    first_row = lax.axis_index("tile") * rows
    first_wave = wave_pos * waves
    chunk = lax.rem(wave_pos + shift, sources // pair)
    count = [counts[first_wave + w] for w in range(waves)]
    limit = functools.reduce(jnp.maximum, count)
    ids = lax.broadcasted_iota(jnp.int32, (SUB, LANES), 0)
    lanes = lax.broadcasted_iota(jnp.int32, (SUB, LANES), 1)

    def spot_of(r):
        return pl.ds(pl.multiple_of(r * SUB, SUB), SUB)

    for w in range(waves):
        for ref, start in ((lo, 0), (own, halo), (hi, halo + rows)):
            for tile in range(ref.shape[2] // SUB):
                base = start + tile * SUB
                scaled = root[w, pl.ds(base, SUB), :]
                for s in range(pair):
                    part = ref[w, chunk * pair + s, pl.ds(tile * SUB, SUB), :].astype(jnp.float32)
                    part = part * scaled
                    for j in range(width):
                        u_even[j, pl.ds(base * SUB + w * pair + s, SUB, stride=SUB), :] = (
                            part[:, j * LANES:(j + 1) * LANES]
                        )
    out[...] = jnp.zeros(out.shape, jnp.float32)
    inject[...] = jnp.zeros(inject.shape, jnp.float32)
    for s in range(pair):
        for pole, sign in ((0, 1.0), (1, -1.0)):
            r = cells[pairs[chunk * pair + s, pole]] - first_row + halo

            @pl.when(jnp.logical_and(r >= 0, r < tall))
            def _():
                here = spot_of(r)
                add = jnp.where(lax.rem(ids, pair) == s, q_first[here, :], 0.0)
                inject[here, :] = inject[here, :] + sign * add

    def level(t, src, dst, first):
        depth = limit - t
        begin = halo - depth
        boost = pick([0.0, CURRENT / DELTA] + [2.0 * CURRENT / DELTA * v for v in TABLE[1:ITERS]], t)

        def row(r):
            here, above, below = spot_of(r), spot_of(r - 1), spot_of(r + 1)
            mid = [src[j, here, :] for j in range(width)]
            east = [c_east[j, here, :] for j in range(width)]
            left = [pltpu.roll(v, LANES - 1, 1) for v in mid]
            right = [pltpu.roll(e * v, 1, 1) for e, v in zip(east, mid)]
            for j in range(width):
                from_east = left[j] if j == width - 1 else jnp.where(lanes == LANES - 1, left[j + 1], left[j])
                from_west = jnp.where(lanes == 0, right[j - 1], right[j])
                total = (
                    (c_north[j, here, :] * src[j, above, :] + c_north[j, below, :] * src[j, below, :])
                    + (east[j] * from_east + from_west)
                )
                total = total + DIAG * mid[j]
                if first:
                    total = 0.5 * total
                else:
                    total = total - dst[j, here, :]
                if j == 0:
                    total = total + boost * inject[here, :]
                dst[j, here, :] = total

        def body(k, carry):
            for i in range(UNROLL):
                row(begin + UNROLL * k + i)
            return carry

        total_rows = rows + 2 * depth
        lax.fori_loop(0, total_rows // UNROLL, body, 0)
        if UNROLL == 4:

            @pl.when(lax.rem(total_rows, 4) == 2)
            def _():
                row(begin + total_rows - 2)
                row(begin + total_rows - 1)

        for w in range(waves):

            @pl.when(count[w] == t)
            def _():
                gain = weights[first_wave + w] * pick([0.0] + [1.0 / v for v in TABLE[1:ITERS + 1]], t)
                for tile in range(rows // SUB):
                    base = halo + tile * SUB
                    for j in range(width):
                        cut = pl.ds(j * LANES, LANES)
                        factor = gain * inverse[w, pl.ds(tile * SUB, SUB), cut]
                        for s in range(pair):
                            at = pl.ds(base * SUB + w * pair + s, SUB, stride=SUB)
                            here = (s, pl.ds(tile * SUB, SUB), cut)
                            out[here] = out[here] + factor * dst[j, at, :]

    level(1, u_even, u_odd, True)

    def two(k, _):
        level(2 * k, u_odd, u_even, False)

        @pl.when(2 * k + 1 <= limit)
        def _():
            level(2 * k + 1, u_even, u_odd, False)

        return 0

    lax.fori_loop(1, limit // 2 + 1, two, 0)


def local(
    initial_fields, conductivity, wavenumbers, quad_weights, sweep_counts, electrode_cells,
    source_pairs,
):
    rows, cols = conductivity.shape
    waves, sources = initial_fields.shape[:2]
    halo = ITERS
    groups = lax.axis_size("wave")
    pair = sources // groups
    count = lax.axis_size("tile")
    forward = [(i, i + 1) for i in range(count - 1)]
    backward = [(i + 1, i) for i in range(count - 1)]
    cond_lo = lax.ppermute(conductivity[-halo:], "tile", forward)
    cond_hi = lax.ppermute(conductivity[:halo], "tile", backward)
    lo = lax.ppermute(initial_fields[:, :, -halo:], "tile", forward)
    hi = lax.ppermute(initial_fields[:, :, :halo], "tile", backward)
    tall = rows + 2 * halo
    width = cols // LANES
    smem = pl.BlockSpec(memory_space=pltpu.SMEM)
    vmem = pl.BlockSpec(memory_space=pltpu.VMEM)
    f32 = lambda *shape: jax.ShapeDtypeStruct(shape, jnp.float32)
    coefficients = pl.pallas_call(
        coefficients_kernel,
        out_shape=(
            f32(width, tall * SUB, LANES), f32(width, tall * SUB, LANES), f32(waves, tall, cols),
            f32(waves, rows, cols), f32(tall * SUB, LANES),
        ),
        in_specs=[smem, vmem, vmem, vmem],
        out_specs=[vmem] * 5,
        scratch_shapes=[
            pltpu.VMEM((tall + 2 * halo, cols), jnp.float32),
            pltpu.VMEM((waves, tall + halo, cols), jnp.float32),
        ],
        compiler_params=pltpu.CompilerParams(vmem_limit_bytes=16 << 20),
        cost_estimate=pl.CostEstimate(flops=4000000, bytes_accessed=6000000, transcendentals=0),
        name="coefficients",
    )(wavenumbers, cond_lo, conductivity, cond_hi)
    total = None
    shifts = [groups // 2] + [j for j in range(1, groups) if j != groups // 2] + [0]
    arrived = []
    for shift in shifts:
        part = pl.pallas_call(
            functools.partial(sweep_kernel, shift),
            out_shape=f32(pair, rows, cols),
            in_specs=[smem] * 4 + [vmem] * 8,
            out_specs=vmem,
            scratch_shapes=[pltpu.VMEM((width, tall * SUB, LANES), jnp.float32)] * 2
            + [pltpu.VMEM((tall * SUB, LANES), jnp.float32)],
            compiler_params=pltpu.CompilerParams(vmem_limit_bytes=20 << 20),
            cost_estimate=pl.CostEstimate(flops=100000000, bytes_accessed=6000000, transcendentals=0),
            name=f"sweeps_{shift}",
        )(sweep_counts, quad_weights, electrode_cells, source_pairs, lo, initial_fields, hi, *coefficients)
        if shift:
            ring = [(i, (i + shift) % groups) for i in range(groups)]
            part = lax.ppermute(part, "wave", ring)
        arrived.append(part)
    return sum(arrived[1:], arrived[0])


def solution(mesh):
    placed = (P("wave", None, "tile", None), P("tile", None), P(), P(), P(), P(), P())
    return jax.shard_map(
        local, mesh=mesh, in_specs=placed, out_specs=P("wave", "tile", None), check_vma=False
    )
```

```python
import functools

import jax
import jax.numpy as jnp
from jax import lax
from jax.experimental import pallas as pl
from jax.experimental.pallas import tpu as pltpu
from jax.sharding import PartitionSpec as P

ITERS = 8
LOWER = 0.1
UPPER = 2.0
THETA = (UPPER + LOWER) / 2.0
DELTA = (UPPER - LOWER) / 2.0
SIGMA_ONE = THETA / DELTA
CURRENT = 2.0
DIAG = 2.0 * (THETA - 1.0) / DELTA
LANES = 128
SUB = 8
UNROLL = 4


def chebyshev_table():
    values = [1.0, SIGMA_ONE]
    for _ in range(ITERS):
        values.append(2.0 * SIGMA_ONE * values[-1] - values[-2])
    return values


TABLE = chebyshev_table()


def pick(values, t):
    result = jnp.float32(values[0])
    for k in range(1, len(values)):
        result = jnp.where(t == k, jnp.float32(values[k]), result)
    return result


def exchange(values, lanes):
    values = list(values)
    step = len(values) // 2
    while step:
        upper = lax.rem(lax.div(lanes, step), 2) == 1
        for i in range(len(values)):
            if i & step:
                continue
            low, high = values[i], values[i + step]
            values[i] = jnp.where(upper, pltpu.roll(high, step, 1), low)
            values[i + step] = jnp.where(upper, high, pltpu.roll(low, LANES - step, 1))
        step //= 2
    return values


def wrap_west(value, lanes, span):
    return jnp.where(
        lanes < span, pltpu.roll(value, span + 1, 1), pltpu.roll(value, span, 1)
    )


def wrap_east(value, lanes, span):
    return jnp.where(
        lanes >= LANES - span, pltpu.roll(value, LANES - span - 1, 1),
        pltpu.roll(value, LANES - span, 1),
    )


def pieces(value):
    return [value[:, j:j + LANES] for j in range(0, value.shape[1], LANES)]


def coefficients_kernel(
    wavenumbers, cond_lo, cond, cond_hi,
    c_north, c_east, c_wrap, root, inverse, q_first, cond_pad, q_pad,
):
    rows, cols = cond.shape
    halo = cond_lo.shape[0]
    waves, width = root.shape[:2]
    tall = rows + 2 * halo
    pair = SUB // waves
    first = lax.axis_index("wave") * waves
    lanes = lax.broadcasted_iota(jnp.int32, (SUB, LANES), 1)
    squares = [wavenumbers[first + w] * wavenumbers[first + w] for w in range(waves)]
    blank = jnp.zeros((SUB, LANES), jnp.float32)

    def store(at, value):
        for j, part in enumerate(exchange(pieces(value), lanes)):
            cond_pad[j, pl.ds(at, SUB), :] = part

    for j in range(width):
        cond_pad[j, pl.ds(0, SUB), :] = blank
        cond_pad[j, pl.ds(SUB + tall, SUB), :] = blank
        for w in range(waves):
            q_pad[w, j, pl.ds(0, SUB), :] = blank
    store(SUB, cond_lo[...])
    store(SUB + halo + rows, cond_hi[...])

    def own(k, carry):
        store(pl.multiple_of(SUB + halo + k * SUB, SUB), cond[pl.ds(pl.multiple_of(k * SUB, SUB), SUB), :])
        return carry

    lax.fori_loop(0, rows // SUB, own, 0)

    def tile(k, carry):
        base = pl.multiple_of(k * SUB, SUB)
        plain = pl.ds(base, SUB)
        mid = [cond_pad[j, pl.ds(base + SUB, SUB), :] for j in range(width)]
        north, east, diagonal = [], [], []
        for j in range(width):
            up = cond_pad[j, pl.ds(base + SUB - 1, SUB), :]
            down = cond_pad[j, pl.ds(base + SUB + 1, SUB), :]
            if j + 1 < width:
                right = mid[j + 1]
            else:
                right = jnp.where(lanes == LANES - 1, 0.0, wrap_east(mid[0], lanes, width))
            left = mid[j - 1] if j else jnp.where(lanes == 0, 0.0, wrap_west(mid[-1], lanes, width))
            north.append(0.5 * (mid[j] + up))
            east.append(0.5 * (mid[j] + right))
            diagonal.append(north[j] + 0.5 * (mid[j] + down) + 0.5 * (mid[j] + left) + east[j])
        east[-1] = jnp.where(lanes == LANES - 1, 0.0, east[-1])
        for w in range(waves):
            q = []
            for j in range(width):
                sq = jnp.sqrt(diagonal[j] + squares[w] * mid[j])
                root[w, j, plain, :] = sq
                q.append(jnp.where(mid[j] > 0.0, 1.0 / sq, 0.0))
                inverse[w, j, plain, :] = q[j]
                q_pad[w, j, pl.ds(base + SUB, SUB), :] = q[j]
            for j in range(width):
                right = q[j + 1] if j + 1 < width else wrap_east(q[0], lanes, width)
                scaled = (2.0 / DELTA) * q[j]
                north_w = scaled * q_pad[w, j, pl.ds(base + SUB - 1, SUB), :] * north[j]
                east_w = scaled * right * east[j]
                for s in range(pair):
                    spot = pl.ds((base + 1) * SUB + w * pair + s, SUB, stride=SUB)
                    c_north[j, spot, :] = north_w
                    c_east[j, spot, :] = east_w
                    if j == 0:
                        q_first[spot, :] = jnp.where(lanes == 0, q[0], 0.0)
                    if j == width - 1:
                        c_wrap[spot, :] = jnp.where(lanes == 0, 0.0, wrap_west(east_w, lanes, width))
        return carry

    lax.fori_loop(0, tall // SUB, tile, 0)


def sweep_kernel(
    shift, counts, weights, cells, pairs,
    lo, own, hi, c_north, c_east, c_wrap, root, inverse, q_first,
    out, u_even, u_odd, inject,
):
    waves, sources, rows, cols = own.shape
    halo = lo.shape[2]
    pair = out.shape[0]
    tall = rows + 2 * halo
    width = cols // LANES
    wave_pos = lax.axis_index("wave")
    first_row = lax.axis_index("tile") * rows
    first_wave = wave_pos * waves
    chunk = lax.rem(wave_pos + shift, sources // pair)
    count = [counts[first_wave + w] for w in range(waves)]
    limit = functools.reduce(jnp.maximum, count)
    least = functools.reduce(jnp.minimum, count)
    ids = lax.broadcasted_iota(jnp.int32, (SUB, LANES), 0)
    lanes = lax.broadcasted_iota(jnp.int32, (SUB, LANES), 1)
    count_of = functools.reduce(
        lambda v, w: jnp.where(lax.div(ids, pair) == w, count[w], v), range(waves), jnp.zeros_like(ids)
    )

    def spot_of(r):
        return pl.ds(pl.multiple_of(r * SUB, SUB), SUB)

    def begin_tile(base, load):
        for w in range(waves):
            for s in range(pair):
                for j, part in enumerate(exchange(pieces(load(w, chunk * pair + s)), lanes)):
                    spot = pl.ds((base + 1) * SUB + w * pair + s, SUB, stride=SUB)
                    u_even[j, spot, :] = part * root[w, j, pl.ds(base, SUB), :]

    def begin_own(k, carry):
        at = pl.ds(pl.multiple_of(k * SUB, SUB), SUB)
        begin_tile(
            pl.multiple_of(halo + k * SUB, SUB), lambda w, c: own[w, c, at, :].astype(jnp.float32)
        )
        return carry

    def begin_ends(k, carry):
        begin_tile(
            pl.multiple_of(k * (halo + rows), SUB),
            lambda w, c: jnp.where(k == 0, lo[w, c].astype(jnp.float32), hi[w, c].astype(jnp.float32)),
        )
        return carry

    lax.fori_loop(0, rows // SUB, begin_own, 0)
    lax.fori_loop(0, 2, begin_ends, 0)

    def wipe(k, carry):
        inject[spot_of(k), :] = jnp.zeros((SUB, LANES), jnp.float32)
        return carry

    lax.fori_loop(0, tall + 2, wipe, 0)
    for s in range(pair):
        for pole, sign in ((0, 1.0), (1, -1.0)):
            r = cells[pairs[chunk * pair + s, pole]] - first_row + halo

            @pl.when(jnp.logical_and(r >= 0, r < tall))
            def _():
                here = spot_of(r + 1)
                add = jnp.where(lax.rem(ids, pair) == s, q_first[here, :], 0.0)
                inject[here, :] = inject[here, :] + sign * add

    def level(t, src, dst, first):
        depth = limit - t + lax.rem(limit - t, 2)
        begin = halo - depth + 1
        boost = pick([0.0, CURRENT / DELTA] + [2.0 * CURRENT / DELTA * v for v in TABLE[1:ITERS]], t)
        live = count_of >= t

        def group(r, size, masked):
            spots = [spot_of(r + i - 1) for i in range(size + 2)]
            inner = range(1, size + 1)
            load = lambda ref, j, many: {i: ref[j, spots[i], :] for i in many}
            around = range(size + 2)
            start = load(src, 0, around)
            final = load(src, width - 1, around)
            past = {i: c_wrap[spots[i], :] * wrap_west(final[i], lanes, width) for i in inner}
            mid = start
            for j in range(width):
                if j + 1 < width - 1:
                    after = load(src, j + 1, around)
                elif j + 1 == width - 1:
                    after = final
                else:
                    after = {i: wrap_east(start[i], lanes, width) for i in inner}
                north = load(c_north, j, range(1, size + 2))
                east = load(c_east, j, inner)
                before = past
                past = {i: east[i] * mid[i] for i in inner}
                for i in inner:
                    total = (
                        (north[i] * mid[i - 1] + north[i + 1] * mid[i + 1])
                        + (east[i] * after[i] + before[i])
                    )
                    if first:
                        total = 0.5 * (total + DIAG * mid[i])
                    else:
                        total = total + (DIAG * mid[i] - dst[j, spots[i], :])
                    if j == 0:
                        total = total + boost * inject[spots[i], :]
                    if masked:
                        total = jnp.where(live, total, mid[i])
                    dst[j, spots[i], :] = total
                mid = after

        def loop(masked):
            def body(k, carry):
                group(begin + UNROLL * k, UNROLL, masked)
                return carry

            lax.fori_loop(0, (rows + 2 * depth) // UNROLL, body, 0)

        if first:
            loop(False)
        else:
            pl.when(t <= least)(lambda: loop(False))
            pl.when(t > least)(lambda: loop(True))

    level(1, u_even, u_odd, True)

    def two(k, carry):
        level(2 * k, u_odd, u_even, False)
        pl.when(2 * k + 1 <= limit)(lambda: level(2 * k + 1, u_even, u_odd, False))
        return carry

    lax.fori_loop(1, lax.div(limit, 2) + 1, two, 0)
    ends = [0.0] + [1.0 / v for v in TABLE[1:ITERS + 1]]
    gains = [weights[first_wave + w] * pick(ends, count[w]) for w in range(waves)]

    def finish(last):
        def body(k, carry):
            at = pl.multiple_of(k * SUB, SUB)
            base = at + halo
            for s in range(pair):
                sums = []
                for j in range(width):
                    terms = [
                        (gains[w] * inverse[w, j, pl.ds(base, SUB), :])
                        * last[j, pl.ds((base + 1) * SUB + w * pair + s, SUB, stride=SUB), :]
                        for w in range(waves)
                    ]
                    sums.append(functools.reduce(jnp.add, terms))
                for j, part in enumerate(exchange(sums, lanes)):
                    out[s, pl.ds(at, SUB), pl.ds(j * LANES, LANES)] = part
            return carry

        lax.fori_loop(0, rows // SUB, body, 0)

    pl.when(lax.rem(limit, 2) == 0)(lambda: finish(u_even))
    pl.when(lax.rem(limit, 2) == 1)(lambda: finish(u_odd))


def local(
    initial_fields, conductivity, wavenumbers, quad_weights, sweep_counts, electrode_cells,
    source_pairs,
):
    rows, cols = conductivity.shape
    waves, sources = initial_fields.shape[:2]
    halo = ITERS
    groups = lax.axis_size("wave")
    pair = sources // groups
    count = lax.axis_size("tile")
    forward = [(i, i + 1) for i in range(count - 1)]
    backward = [(i + 1, i) for i in range(count - 1)]
    cond_lo = lax.ppermute(conductivity[-halo:], "tile", forward)
    cond_hi = lax.ppermute(conductivity[:halo], "tile", backward)
    lo = lax.ppermute(initial_fields[:, :, -halo:], "tile", forward)
    hi = lax.ppermute(initial_fields[:, :, :halo], "tile", backward)
    tall = rows + 2 * halo
    width = cols // LANES
    high = (tall + 2) * SUB
    smem = pl.BlockSpec(memory_space=pltpu.SMEM)
    vmem = pl.BlockSpec(memory_space=pltpu.VMEM)
    f32 = lambda *shape: jax.ShapeDtypeStruct(shape, jnp.float32)
    coefficients = pl.pallas_call(
        coefficients_kernel,
        out_shape=(
            f32(width, high, LANES), f32(width, high, LANES), f32(high, LANES),
            f32(waves, width, tall, LANES), f32(waves, width, tall, LANES), f32(high, LANES),
        ),
        in_specs=[smem, vmem, vmem, vmem],
        out_specs=[vmem] * 6,
        scratch_shapes=[
            pltpu.VMEM((width, tall + 2 * SUB, LANES), jnp.float32),
            pltpu.VMEM((waves, width, tall + SUB, LANES), jnp.float32),
        ],
        compiler_params=pltpu.CompilerParams(vmem_limit_bytes=16 << 20),
        cost_estimate=pl.CostEstimate(flops=4000000, bytes_accessed=6000000, transcendentals=0),
        name="coefficients",
    )(wavenumbers, cond_lo, conductivity, cond_hi)
    total = None
    shifts = [groups // 2] + [j for j in range(1, groups) if j != groups // 2] + [0]
    arrived = []
    for shift in shifts:
        part = pl.pallas_call(
            functools.partial(sweep_kernel, shift),
            out_shape=f32(pair, rows, cols),
            in_specs=[smem] * 4 + [vmem] * 9,
            out_specs=vmem,
            scratch_shapes=[pltpu.VMEM((width, high, LANES), jnp.float32)] * 2
            + [pltpu.VMEM((high, LANES), jnp.float32)],
            compiler_params=pltpu.CompilerParams(vmem_limit_bytes=20 << 20),
            cost_estimate=pl.CostEstimate(flops=100000000, bytes_accessed=6000000, transcendentals=0),
            name=f"sweeps_{shift}",
        )(sweep_counts, quad_weights, electrode_cells, source_pairs, lo, initial_fields, hi, *coefficients)
        if shift:
            ring = [(i, (i + shift) % groups) for i in range(groups)]
            part = lax.ppermute(part, "wave", ring)
        arrived.append(part)
    return sum(arrived[1:], arrived[0])


def solution(mesh):
    placed = (P("wave", None, "tile", None), P("tile", None), P(), P(), P(), P(), P())
    return jax.shard_map(
        local, mesh=mesh, in_specs=placed, out_specs=P("wave", "tile", None), check_vma=False
    )
```

```python
import functools

import jax
import jax.numpy as jnp
from jax import lax
from jax.experimental import pallas as pl
from jax.experimental.pallas import tpu as pltpu
from jax.sharding import PartitionSpec as P


ITERS = 8
LOWER = 0.1
UPPER = 2.0
THETA = (UPPER + LOWER) / 2.0
DELTA = (UPPER - LOWER) / 2.0
SIGMA_ONE = THETA / DELTA
CURRENT = 2.0
DIAG = 2.0 * (THETA - 1.0) / DELTA
LANES = 128
SUB = 8
UNROLL = 4
PLANES = 3


def chebyshev_table():
    values = [1.0, SIGMA_ONE]
    for _ in range(ITERS):
        values.append(2.0 * SIGMA_ONE * values[-1] - values[-2])
    return values


TABLE = chebyshev_table()


def pick(values, t):
    result = jnp.float32(values[0])
    for k in range(1, len(values)):
        result = jnp.where(t == k, jnp.float32(values[k]), result)
    return result


def exchange(values, lanes):
    values = list(values)
    step = len(values) // 2
    while step:
        upper = lax.rem(lax.div(lanes, step), 2) == 1
        for i in range(len(values)):
            if i & step:
                continue
            low, high = values[i], values[i + step]
            values[i] = jnp.where(upper, pltpu.roll(high, step, 1), low)
            values[i + step] = jnp.where(upper, high, pltpu.roll(low, LANES - step, 1))
        step //= 2
    return values


def wrap_west(value, lanes, span):
    return jnp.take_along_axis(
        value, jnp.where(lanes < span, lanes + (LANES - span - 1), lanes - span), axis=1,
        mode="promise_in_bounds",
    )


def wrap_east(value, lanes, span):
    return jnp.take_along_axis(
        value, jnp.where(lanes < LANES - span, lanes + span, lanes - (LANES - span - 1)), axis=1,
        mode="promise_in_bounds",
    )


def pieces(value):
    return [value[:, j:j + LANES] for j in range(0, value.shape[1], LANES)]


def coefficients_kernel(
    wavenumbers, near, cond, across,
    c_north, c_east, c_wrap, root, inverse, q_first, cond_pad, q_pad,
):
    rows, _ = cond.shape
    halo = near.shape[1]
    waves, width = root.shape[:2]
    tall = rows + 2 * halo
    pair = SUB // waves
    first = lax.axis_index("wave") * waves
    lanes = lax.broadcasted_iota(jnp.int32, (SUB, LANES), 1)
    squares = [wavenumbers[first + w] * wavenumbers[first + w] for w in range(waves)]
    blank = jnp.zeros((SUB, LANES), jnp.float32)

    def store(at, value):
        for j, part in enumerate(exchange(pieces(value), lanes)):
            cond_pad[j, pl.ds(at, SUB), :] = part

    for j in range(width):
        cond_pad[j, pl.ds(0, SUB), :] = blank
        cond_pad[j, pl.ds(SUB + tall, SUB), :] = blank
        for w in range(waves):
            q_pad[w, j, pl.ds(0, SUB), :] = blank
    low = lax.rem(lax.axis_index("tile"), 2) == 0
    for ref, at in (
        (near, jnp.where(low, SUB + halo + rows, SUB)),
        (across, jnp.where(low, SUB, SUB + halo + rows)),
    ):
        planes = [ref[SUB + i].astype(jnp.float32) for i in range(PLANES)]
        store(pl.multiple_of(at, SUB), functools.reduce(jnp.add, planes))

    def own(k, carry):
        store(pl.multiple_of(SUB + halo + k * SUB, SUB), cond[pl.ds(pl.multiple_of(k * SUB, SUB), SUB), :])
        return carry

    lax.fori_loop(0, rows // SUB, own, 0)

    def tile(k, carry):
        base = pl.multiple_of(k * SUB, SUB)
        plain = pl.ds(base, SUB)
        mid = [cond_pad[j, pl.ds(base + SUB, SUB), :] for j in range(width)]
        north, east, diagonal = [], [], []
        for j in range(width):
            up = cond_pad[j, pl.ds(base + SUB - 1, SUB), :]
            down = cond_pad[j, pl.ds(base + SUB + 1, SUB), :]
            if j + 1 < width:
                right = mid[j + 1]
            else:
                right = jnp.where(lanes == LANES - 1, 0.0, wrap_east(mid[0], lanes, width))
            left = mid[j - 1] if j else jnp.where(lanes == 0, 0.0, wrap_west(mid[-1], lanes, width))
            north.append(0.5 * (mid[j] + up))
            east.append(0.5 * (mid[j] + right))
            diagonal.append(north[j] + 0.5 * (mid[j] + down) + 0.5 * (mid[j] + left) + east[j])
        east[-1] = jnp.where(lanes == LANES - 1, 0.0, east[-1])
        for w in range(waves):
            q = []
            for j in range(width):
                full = diagonal[j] + squares[w] * mid[j]
                q.append(jnp.where(mid[j] > 0.0, lax.rsqrt(full), 0.0))
                root[w, j, plain, :] = full * q[j]
                inverse[w, j, plain, :] = q[j]
                q_pad[w, j, pl.ds(base + SUB, SUB), :] = q[j]
            for j in range(width):
                right = q[j + 1] if j + 1 < width else wrap_east(q[0], lanes, width)
                scaled = (2.0 / DELTA) * q[j]
                north_w = scaled * q_pad[w, j, pl.ds(base + SUB - 1, SUB), :] * north[j]
                east_w = scaled * right * east[j]
                for s in range(pair):
                    spot = pl.ds((base + 1) * SUB + w * pair + s, SUB, stride=SUB)
                    c_north[j, spot, :] = north_w
                    c_east[j, spot, :] = east_w
                    if j == 0:
                        q_first[spot, :] = jnp.where(lanes == 0, q[0], 0.0)
                    if j == width - 1:
                        c_wrap[spot, :] = jnp.where(lanes == 0, 0.0, wrap_west(east_w, lanes, width))
        return carry

    lax.fori_loop(0, tall // SUB, tile, 0)


def pack_kernel(order, fields, cond, near, across, near_rest, across_rest, edge, edge_sems, sems):
    waves, sources, rows, _ = fields.shape
    groups = len(order)
    pair = sources // groups
    halo = near.shape[1]
    wave_pos = lax.axis_index("wave")
    low = lax.rem(lax.axis_index("tile"), 2) == 0
    ends = jnp.where(low, rows - halo, 0), jnp.where(low, 0, rows - halo)
    edges = [
        pltpu.make_async_copy(
            cond.at[pl.ds(pl.multiple_of(end, halo), halo), :], edge.at[i], edge_sems.at[i]
        )
        for i, end in enumerate(ends)
    ]
    for copy in edges:
        copy.start()
    copies = []
    for k, shift in enumerate(order):
        chunk = lax.rem(wave_pos + shift, groups)
        for (first, rest), end in zip(((across, across_rest), (near, near_rest)), ends[::-1]):
            for w in range(waves):
                source = fields.at[
                    w, pl.ds(chunk * pair, pair), pl.ds(pl.multiple_of(end, halo), halo), :
                ]
                if k == 0:
                    target = first.at[pl.ds(w * pair, pair)]
                else:
                    target = rest.at[pl.ds((w * (groups - 1) + k - 1) * pair, pair)]
                copies.append(pltpu.make_async_copy(source, target, sems.at[len(copies)]))
    for copy in copies:
        copy.start()
    for k, ref in enumerate((near, across)):
        edges[k].wait()
        value = edge[k]
        for i in range(PLANES):
            part = value.astype(jnp.bfloat16)
            ref[SUB + i] = part
            value = value - part.astype(jnp.float32)
    for copy in copies:
        copy.wait()


def sweep_kernel(
    shift, place, counts, weights, cells, pairs,
    near, own, across, c_north, c_east, c_wrap, root, inverse, q_first,
    out, u_even, u_odd, inject,
):
    waves, sources, rows, cols = own.shape
    halo = near.shape[1]
    pair = out.shape[0]
    per, skip = place
    tall = rows + 2 * halo
    width = cols // LANES
    wave_pos = lax.axis_index("wave")
    first_row = lax.axis_index("tile") * rows
    first_wave = wave_pos * waves
    chunk = lax.rem(wave_pos + shift, sources // pair)
    count = [counts[first_wave + w] for w in range(waves)]
    limit = functools.reduce(jnp.maximum, count)
    least = functools.reduce(jnp.minimum, count)
    ids = lax.broadcasted_iota(jnp.int32, (SUB, LANES), 0)
    lanes = lax.broadcasted_iota(jnp.int32, (SUB, LANES), 1)
    count_of = functools.reduce(
        lambda v, w: jnp.where(lax.div(ids, pair) == w, count[w], v), range(waves), jnp.zeros_like(ids)
    )

    def spot_of(r):
        return pl.ds(pl.multiple_of(r * SUB, SUB), SUB)

    wide = lax.broadcasted_iota(jnp.int32, (2 * SUB, LANES), 1)

    def begin_tile(bases, load):
        for w in range(waves):
            for s in range(pair):
                for j, part in enumerate(exchange(pieces(load(w, s)), wide)):
                    part = part.astype(jnp.float32)
                    for half, base in enumerate(bases):
                        spot = pl.ds((base + 1) * SUB + w * pair + s, SUB, stride=SUB)
                        u_even[j, spot, :] = (
                            part[half * SUB:(half + 1) * SUB] * root[w, j, pl.ds(base, SUB), :]
                        )

    def begin_own(k, carry):
        at = pl.multiple_of(k * 2 * SUB, 2 * SUB)
        base = pl.multiple_of(halo + at, SUB)
        begin_tile((base, base + SUB), lambda w, s: own[w, chunk * pair + s, pl.ds(at, 2 * SUB), :])
        return carry

    lax.fori_loop(0, rows // (2 * SUB), begin_own, 0)
    low = lax.rem(lax.axis_index("tile"), 2) == 0
    begin_tile(
        (
            pl.multiple_of(jnp.where(low, halo + rows, 0), SUB),
            pl.multiple_of(jnp.where(low, 0, halo + rows), SUB),
        ),
        lambda w, s: jnp.concatenate([ref[w * per + skip + s] for ref in (near, across)], axis=0),
    )

    def wipe(k, carry):
        inject[spot_of(k), :] = jnp.zeros((SUB, LANES), jnp.float32)
        return carry

    lax.fori_loop(0, tall + 2, wipe, 0)
    for s in range(pair):
        for pole, sign in ((0, 1.0), (1, -1.0)):
            r = cells[pairs[chunk * pair + s, pole]] - first_row + halo

            @pl.when(jnp.logical_and(r >= 0, r < tall))
            def _():
                here = spot_of(r + 1)
                add = jnp.where(lax.rem(ids, pair) == s, q_first[here, :], 0.0)
                inject[here, :] = inject[here, :] + sign * add

    def level(t, src, dst, first):
        depth = limit - t + lax.rem(limit - t, 2)
        begin = halo - depth + 1
        boost = pick([0.0, CURRENT / DELTA] + [2.0 * CURRENT / DELTA * v for v in TABLE[1:ITERS]], t)
        live = count_of >= t

        def group(r, size, masked):
            spots = [spot_of(r + i - 1) for i in range(size + 2)]
            inner = range(1, size + 1)
            load = lambda ref, j, many: {i: ref[j, spots[i], :] for i in many}
            around = range(size + 2)
            start = load(src, 0, around)
            final = load(src, width - 1, around)
            past = {i: c_wrap[spots[i], :] * wrap_west(final[i], lanes, width) for i in inner}
            mid = start
            for j in range(width):
                if j + 1 < width - 1:
                    after = load(src, j + 1, around)
                elif j + 1 == width - 1:
                    after = final
                else:
                    after = {i: wrap_east(start[i], lanes, width) for i in inner}
                north = load(c_north, j, range(1, size + 2))
                east = load(c_east, j, inner)
                before = past
                past = {i: east[i] * mid[i] for i in inner}
                for i in inner:
                    total = (
                        (north[i] * mid[i - 1] + north[i + 1] * mid[i + 1])
                        + (east[i] * after[i] + before[i])
                    )
                    if first:
                        total = 0.5 * (total + DIAG * mid[i])
                    else:
                        total = total + (DIAG * mid[i] - dst[j, spots[i], :])
                    if j == 0:
                        total = total + boost * inject[spots[i], :]
                    if masked:
                        total = jnp.where(live, total, mid[i])
                    dst[j, spots[i], :] = total
                mid = after

        def loop(masked):
            def body(k, carry):
                group(begin + UNROLL * k, UNROLL, masked)
                return carry

            lax.fori_loop(0, (rows + 2 * depth) // UNROLL, body, 0)

        if first:
            loop(False)
        else:
            pl.when(t <= least)(lambda: loop(False))
            pl.when(t > least)(lambda: loop(True))

    level(1, u_even, u_odd, True)

    def two(k, carry):
        level(2 * k, u_odd, u_even, False)
        pl.when(2 * k + 1 <= limit)(lambda: level(2 * k + 1, u_even, u_odd, False))
        return carry

    lax.fori_loop(1, lax.div(limit, 2) + 1, two, 0)
    ends = [0.0] + [1.0 / v for v in TABLE[1:ITERS + 1]]
    gains = [weights[first_wave + w] * pick(ends, count[w]) for w in range(waves)]

    def finish(last):
        def body(k, carry):
            at = pl.multiple_of(k * SUB, SUB)
            base = at + halo
            for s in range(pair):
                sums = []
                for j in range(width):
                    terms = [
                        (gains[w] * inverse[w, j, pl.ds(base, SUB), :])
                        * last[j, pl.ds((base + 1) * SUB + w * pair + s, SUB, stride=SUB), :]
                        for w in range(waves)
                    ]
                    sums.append(functools.reduce(jnp.add, terms))
                for j, part in enumerate(exchange(sums, lanes)):
                    out[s, pl.ds(at, SUB), pl.ds(j * LANES, LANES)] = part
            return carry

        lax.fori_loop(0, rows // SUB, body, 0)

    pl.when(lax.rem(limit, 2) == 0)(lambda: finish(u_even))
    pl.when(lax.rem(limit, 2) == 1)(lambda: finish(u_odd))


def local(
    initial_fields, conductivity, wavenumbers, quad_weights, sweep_counts, electrode_cells,
    source_pairs,
):
    rows, cols = conductivity.shape
    waves, sources = initial_fields.shape[:2]
    halo = ITERS
    groups = lax.axis_size("wave")
    pair = sources // groups
    count = lax.axis_size("tile")
    order = [groups // 2] + [j for j in range(1, groups) if j != groups // 2] + [0]
    beside = [(i, i ^ 1) for i in range(count)]
    between = [(i, i + 1 if i % 2 else i - 1) for i in range(1, count - 1)]
    smem = pl.BlockSpec(memory_space=pltpu.SMEM)
    vmem = pl.BlockSpec(memory_space=pltpu.VMEM)
    bf16 = lambda *shape: jax.ShapeDtypeStruct(shape, jnp.bfloat16)
    ends = bf16(SUB + PLANES, halo, cols), bf16(SUB * (groups - 1), halo, cols)
    near, across, near_rest, across_rest = pl.pallas_call(
        functools.partial(pack_kernel, order),
        out_shape=(ends[0], ends[0], ends[1], ends[1]),
        in_specs=[pl.BlockSpec(memory_space=pltpu.HBM)] * 2,
        out_specs=[vmem] * 4,
        scratch_shapes=[
            pltpu.VMEM((2, halo, cols), jnp.float32),
            pltpu.SemaphoreType.DMA((2,)),
            pltpu.SemaphoreType.DMA((2 * waves * groups,)),
        ],
        compiler_params=pltpu.CompilerParams(vmem_limit_bytes=8 << 20),
        cost_estimate=pl.CostEstimate(flops=100000, bytes_accessed=2000000, transcendentals=0),
        name="pack",
    )(pltpu.with_memory_space_constraint(initial_fields, pltpu.HBM), pltpu.with_memory_space_constraint(conductivity, pltpu.HBM))
    across = lax.ppermute(across, "tile", between)
    near = lax.ppermute(near, "tile", beside)
    across_rest = lax.ppermute(across_rest, "tile", between)
    near_rest = lax.ppermute(near_rest, "tile", beside)
    tall = rows + 2 * halo
    width = cols // LANES
    high = (tall + 2) * SUB
    f32 = lambda *shape: jax.ShapeDtypeStruct(shape, jnp.float32)
    coefficients = pl.pallas_call(
        coefficients_kernel,
        out_shape=(
            f32(width, high, LANES), f32(width, high, LANES), f32(high, LANES),
            f32(waves, width, tall, LANES), f32(waves, width, tall, LANES), f32(high, LANES),
        ),
        in_specs=[smem, vmem, vmem, vmem],
        out_specs=[vmem] * 6,
        scratch_shapes=[
            pltpu.VMEM((width, tall + 2 * SUB, LANES), jnp.float32),
            pltpu.VMEM((waves, width, tall + SUB, LANES), jnp.float32),
        ],
        compiler_params=pltpu.CompilerParams(vmem_limit_bytes=16 << 20),
        cost_estimate=pl.CostEstimate(flops=4000000, bytes_accessed=6000000, transcendentals=0),
        name="coefficients",
    )(wavenumbers, near, conductivity, across)
    arrived = []
    for k, shift in enumerate(order):
        place = ((groups - 1) * pair, (k - 1) * pair) if k else (pair, 0)
        ends = (near_rest, across_rest) if k else (near, across)
        part = pl.pallas_call(
            functools.partial(sweep_kernel, shift, place),
            out_shape=f32(pair, rows, cols),
            in_specs=[smem] * 4 + [vmem] * 9,
            out_specs=vmem,
            scratch_shapes=[pltpu.VMEM((width, high, LANES), jnp.float32)] * 2
            + [pltpu.VMEM((high, LANES), jnp.float32)],
            compiler_params=pltpu.CompilerParams(vmem_limit_bytes=20 << 20),
            cost_estimate=pl.CostEstimate(flops=100000000, bytes_accessed=6000000, transcendentals=0),
        )(sweep_counts, quad_weights, electrode_cells, source_pairs, ends[0], initial_fields, ends[1], *coefficients)
        if shift:
            ring = [(i, (i + shift) % groups) for i in range(groups)]
            part = lax.ppermute(part, "wave", ring)
        arrived.append(part)
    return sum(arrived[1:], arrived[0])


def solution(mesh):
    placed = (P("wave", None, "tile", None), P("tile", None), P(), P(), P(), P(), P())
    return jax.shard_map(
        local, mesh=mesh, in_specs=placed, out_specs=P("wave", "tile", None), check_vma=False
    )
```

```python
import functools

import jax
import jax.numpy as jnp
from jax import lax
from jax.experimental import pallas as pl
from jax.experimental.pallas import tpu as pltpu
from jax.sharding import PartitionSpec as P


ITERS = 8
LOWER = 0.1
UPPER = 2.0
THETA = (UPPER + LOWER) / 2.0
DELTA = (UPPER - LOWER) / 2.0
SIGMA_ONE = THETA / DELTA
CURRENT = 2.0
DIAG = 2.0 * (THETA - 1.0) / DELTA
LANES = 128
SUB = 8
UNROLL = 4
BATCH = 8
PLANES = 3


def chebyshev_table():
    values = [1.0, SIGMA_ONE]
    for _ in range(ITERS):
        values.append(2.0 * SIGMA_ONE * values[-1] - values[-2])
    return values


TABLE = chebyshev_table()


def pick(values, t):
    result = jnp.float32(values[0])
    for k in range(1, len(values)):
        result = jnp.where(t == k, jnp.float32(values[k]), result)
    return result


def exchange(values, lanes):
    values = list(values)
    step = len(values) // 2
    while step:
        upper = lax.rem(lax.div(lanes, step), 2) == 1
        for i in range(len(values)):
            if i & step:
                continue
            low, high = values[i], values[i + step]
            values[i] = jnp.where(upper, pltpu.roll(high, step, 1), low)
            values[i + step] = jnp.where(upper, high, pltpu.roll(low, LANES - step, 1))
        step //= 2
    return values


def wrap_west(value, lanes, span):
    return jnp.take_along_axis(
        value, jnp.where(lanes < span, lanes + (LANES - span - 1), lanes - span), axis=1,
        mode="promise_in_bounds",
    )


def wrap_east(value, lanes, span):
    return jnp.take_along_axis(
        value, jnp.where(lanes < LANES - span, lanes + span, lanes - (LANES - span - 1)), axis=1,
        mode="promise_in_bounds",
    )


def pieces(value):
    return [value[:, j:j + LANES] for j in range(0, value.shape[1], LANES)]


def coefficients_kernel(
    wavenumbers, near, cond, across,
    c_north, c_east, c_wrap, root, inverse, q_first, cond_pad, q_pad,
):
    rows, _ = cond.shape
    halo = near.shape[1]
    waves, width = root.shape[:2]
    tall = rows + 2 * halo
    pair = SUB // waves
    first = lax.axis_index("wave") * waves
    lanes = lax.broadcasted_iota(jnp.int32, (SUB, LANES), 1)
    squares = [wavenumbers[first + w] * wavenumbers[first + w] for w in range(waves)]
    blank = jnp.zeros((SUB, LANES), jnp.float32)

    def store(at, value):
        for j, part in enumerate(exchange(pieces(value), lanes)):
            cond_pad[j, pl.ds(at, SUB), :] = part

    for j in range(width):
        cond_pad[j, pl.ds(0, SUB), :] = blank
        cond_pad[j, pl.ds(SUB + tall, SUB), :] = blank
        for w in range(waves):
            q_pad[w, j, pl.ds(0, SUB), :] = blank
    low = lax.rem(lax.axis_index("tile"), 2) == 0
    for ref, at in (
        (near, jnp.where(low, SUB + halo + rows, SUB)),
        (across, jnp.where(low, SUB, SUB + halo + rows)),
    ):
        planes = [ref[SUB + i].astype(jnp.float32) for i in range(PLANES)]
        store(pl.multiple_of(at, SUB), functools.reduce(jnp.add, planes))

    def own(k, carry):
        store(pl.multiple_of(SUB + halo + k * SUB, SUB), cond[pl.ds(pl.multiple_of(k * SUB, SUB), SUB), :])
        return carry

    lax.fori_loop(0, rows // SUB, own, 0)

    def tile(k, carry):
        base = pl.multiple_of(k * SUB, SUB)
        plain = pl.ds(base, SUB)
        mid = [cond_pad[j, pl.ds(base + SUB, SUB), :] for j in range(width)]
        north, east, diagonal = [], [], []
        for j in range(width):
            up = cond_pad[j, pl.ds(base + SUB - 1, SUB), :]
            down = cond_pad[j, pl.ds(base + SUB + 1, SUB), :]
            if j + 1 < width:
                right = mid[j + 1]
            else:
                right = jnp.where(lanes == LANES - 1, 0.0, wrap_east(mid[0], lanes, width))
            left = mid[j - 1] if j else jnp.where(lanes == 0, 0.0, wrap_west(mid[-1], lanes, width))
            north.append(0.5 * (mid[j] + up))
            east.append(0.5 * (mid[j] + right))
            diagonal.append(north[j] + 0.5 * (mid[j] + down) + 0.5 * (mid[j] + left) + east[j])
        east[-1] = jnp.where(lanes == LANES - 1, 0.0, east[-1])
        for w in range(waves):
            q = []
            for j in range(width):
                full = diagonal[j] + squares[w] * mid[j]
                q.append(jnp.where(mid[j] > 0.0, lax.rsqrt(full), 0.0))
                root[w, j, plain, :] = full * q[j]
                inverse[w, j, plain, :] = q[j]
                q_pad[w, j, pl.ds(base + SUB, SUB), :] = q[j]
            for j in range(width):
                right = q[j + 1] if j + 1 < width else wrap_east(q[0], lanes, width)
                scaled = (2.0 / DELTA) * q[j]
                north_w = scaled * q_pad[w, j, pl.ds(base + SUB - 1, SUB), :] * north[j]
                east_w = scaled * right * east[j]
                for s in range(pair):
                    spot = pl.ds((base + 1) * SUB + w * pair + s, SUB, stride=SUB)
                    c_north[j, spot, :] = north_w
                    c_east[j, spot, :] = east_w
                    if j == 0:
                        q_first[spot, :] = jnp.where(lanes == 0, q[0], 0.0)
                    if j == width - 1:
                        c_wrap[spot, :] = jnp.where(lanes == 0, 0.0, wrap_west(east_w, lanes, width))
        return carry

    lax.fori_loop(0, tall // SUB, tile, 0)


def pack_kernel(order, fields, cond, near, across, near_rest, across_rest, edge, edge_sems, sems):
    waves, sources, rows, _ = fields.shape
    groups = len(order)
    pair = sources // groups
    halo = near.shape[1]
    wave_pos = lax.axis_index("wave")
    low = lax.rem(lax.axis_index("tile"), 2) == 0
    ends = jnp.where(low, rows - halo, 0), jnp.where(low, 0, rows - halo)
    edges = [
        pltpu.make_async_copy(
            cond.at[pl.ds(pl.multiple_of(end, halo), halo), :], edge.at[i], edge_sems.at[i]
        )
        for i, end in enumerate(ends)
    ]
    for copy in edges:
        copy.start()
    copies = []
    for k, shift in enumerate(order):
        chunk = lax.rem(wave_pos + shift, groups)
        for (first, rest), end in zip(((across, across_rest), (near, near_rest)), ends[::-1]):
            for w in range(waves):
                source = fields.at[
                    w, pl.ds(chunk * pair, pair), pl.ds(pl.multiple_of(end, halo), halo), :
                ]
                if k == 0:
                    target = first.at[pl.ds(w * pair, pair)]
                else:
                    target = rest.at[pl.ds((w * (groups - 1) + k - 1) * pair, pair)]
                copies.append(pltpu.make_async_copy(source, target, sems.at[len(copies)]))
    for copy in copies:
        copy.start()
    for k, ref in enumerate((near, across)):
        edges[k].wait()
        value = edge[k]
        for i in range(PLANES):
            part = value.astype(jnp.bfloat16)
            ref[SUB + i] = part
            value = value - part.astype(jnp.float32)
    for copy in copies:
        copy.wait()


def sweep_kernel(
    shift, place, counts, weights, cells, pairs,
    near, own, across, c_north, c_east, c_wrap, root, inverse, q_first,
    out, u_even, u_odd, inject,
):
    waves, sources, rows, cols = own.shape
    halo = near.shape[1]
    pair = out.shape[0]
    per, skip = place
    tall = rows + 2 * halo
    width = cols // LANES
    wave_pos = lax.axis_index("wave")
    first_row = lax.axis_index("tile") * rows
    first_wave = wave_pos * waves
    chunk = lax.rem(wave_pos + shift, sources // pair)
    count = [counts[first_wave + w] for w in range(waves)]
    limit = functools.reduce(jnp.maximum, count)
    least = functools.reduce(jnp.minimum, count)
    ids = lax.broadcasted_iota(jnp.int32, (SUB, LANES), 0)
    lanes = lax.broadcasted_iota(jnp.int32, (SUB, LANES), 1)
    count_of = functools.reduce(
        lambda v, w: jnp.where(lax.div(ids, pair) == w, count[w], v), range(waves), jnp.zeros_like(ids)
    )

    def spot_of(r):
        return pl.ds(pl.multiple_of(r * SUB, SUB), SUB)

    wide = lax.broadcasted_iota(jnp.int32, (2 * SUB, LANES), 1)

    def begin_tile(bases, load):
        for w in range(waves):
            for s in range(pair):
                for j, part in enumerate(exchange(pieces(load(w, s)), wide)):
                    part = part.astype(jnp.float32)
                    for half, base in enumerate(bases):
                        spot = pl.ds((base + 1) * SUB + w * pair + s, SUB, stride=SUB)
                        u_even[j, spot, :] = (
                            part[half * SUB:(half + 1) * SUB] * root[w, j, pl.ds(base, SUB), :]
                        )

    def begin_own(k, carry):
        at = pl.multiple_of(k * 2 * SUB, 2 * SUB)
        base = pl.multiple_of(halo + at, SUB)
        begin_tile((base, base + SUB), lambda w, s: own[w, chunk * pair + s, pl.ds(at, 2 * SUB), :])
        return carry

    lax.fori_loop(0, rows // (2 * SUB), begin_own, 0)
    low = lax.rem(lax.axis_index("tile"), 2) == 0
    begin_tile(
        (
            pl.multiple_of(jnp.where(low, halo + rows, 0), SUB),
            pl.multiple_of(jnp.where(low, 0, halo + rows), SUB),
        ),
        lambda w, s: jnp.concatenate([ref[w * per + skip + s] for ref in (near, across)], axis=0),
    )

    def wipe(k, carry):
        inject[spot_of(k), :] = jnp.zeros((SUB, LANES), jnp.float32)
        return carry

    lax.fori_loop(0, tall + 2, wipe, 0)
    for s in range(pair):
        for pole, sign in ((0, 1.0), (1, -1.0)):
            r = cells[pairs[chunk * pair + s, pole]] - first_row + halo

            @pl.when(jnp.logical_and(r >= 0, r < tall))
            def _():
                here = spot_of(r + 1)
                add = jnp.where(lax.rem(ids, pair) == s, q_first[here, :], 0.0)
                inject[here, :] = inject[here, :] + sign * add

    def level(t, src, dst, first):
        depth = lax.div(limit - t + 3, 4) * 4
        begin = halo - depth + 1
        boost = pick([0.0, CURRENT / DELTA] + [2.0 * CURRENT / DELTA * v for v in TABLE[1:ITERS]], t)
        live = count_of >= t

        def wraps(r, size):
            spots = [spot_of(r + i) for i in range(size)]
            return (
                [wrap_west(src[width - 1, spot, :], lanes, width) for spot in spots]
                + [wrap_east(src[0, spot, :], lanes, width) for spot in spots]
            )

        def group(r, size, masked, turned):
            spots = [spot_of(r + i - 1) for i in range(size + 2)]
            inner = range(1, size + 1)
            load = lambda ref, j, many: {i: ref[j, spots[i], :] for i in many}
            around = range(size + 2)
            past = {i: c_wrap[spots[i], :] * turned[i - 1] for i in inner}
            mid = load(src, 0, around)
            for j in range(width):
                if j + 1 < width:
                    after = load(src, j + 1, around)
                else:
                    after = {i: turned[size + i - 1] for i in inner}
                north = load(c_north, j, range(1, size + 2))
                east = load(c_east, j, inner)
                before = past
                past = {i: east[i] * mid[i] for i in inner}
                for i in inner:
                    total = (
                        (north[i] * mid[i - 1] + north[i + 1] * mid[i + 1])
                        + (east[i] * after[i] + before[i])
                    )
                    if first:
                        total = 0.5 * (total + DIAG * mid[i])
                    else:
                        total = total + (DIAG * mid[i] - dst[j, spots[i], :])
                    if j == 0:
                        total = total + boost * inject[spots[i], :]
                    if masked:
                        total = jnp.where(live, total, mid[i])
                    dst[j, spots[i], :] = total
                mid = after

        def loop(masked):
            def body(k, carry):
                r = begin + BATCH * k
                turned = wraps(r, BATCH)
                for i in range(0, BATCH, UNROLL):
                    group(
                        r + i, UNROLL, masked,
                        turned[i:i + UNROLL] + turned[BATCH + i:BATCH + i + UNROLL],
                    )
                return carry

            lax.fori_loop(0, (rows + 2 * depth) // BATCH, body, 0)

        if first:
            loop(False)
        else:
            pl.when(t <= least)(lambda: loop(False))
            pl.when(t > least)(lambda: loop(True))

    level(1, u_even, u_odd, True)

    def two(k, carry):
        level(2 * k, u_odd, u_even, False)
        pl.when(2 * k + 1 <= limit)(lambda: level(2 * k + 1, u_even, u_odd, False))
        return carry

    lax.fori_loop(1, lax.div(limit, 2) + 1, two, 0)
    ends = [0.0] + [1.0 / v for v in TABLE[1:ITERS + 1]]
    gains = [weights[first_wave + w] * pick(ends, count[w]) for w in range(waves)]

    def finish(last):
        def body(k, carry):
            at = pl.multiple_of(k * SUB, SUB)
            base = at + halo
            for s in range(pair):
                sums = []
                for j in range(width):
                    terms = [
                        (gains[w] * inverse[w, j, pl.ds(base, SUB), :])
                        * last[j, pl.ds((base + 1) * SUB + w * pair + s, SUB, stride=SUB), :]
                        for w in range(waves)
                    ]
                    sums.append(functools.reduce(jnp.add, terms))
                for j, part in enumerate(exchange(sums, lanes)):
                    out[s, pl.ds(at, SUB), pl.ds(j * LANES, LANES)] = part
            return carry

        lax.fori_loop(0, rows // SUB, body, 0)

    pl.when(lax.rem(limit, 2) == 0)(lambda: finish(u_even))
    pl.when(lax.rem(limit, 2) == 1)(lambda: finish(u_odd))


def local(
    initial_fields, conductivity, wavenumbers, quad_weights, sweep_counts, electrode_cells,
    source_pairs,
):
    rows, cols = conductivity.shape
    waves, sources = initial_fields.shape[:2]
    halo = ITERS
    groups = lax.axis_size("wave")
    pair = sources // groups
    count = lax.axis_size("tile")
    order = [groups // 2] + [j for j in range(1, groups) if j != groups // 2] + [0]
    beside = [(i, i ^ 1) for i in range(count)]
    between = [(i, i + 1 if i % 2 else i - 1) for i in range(1, count - 1)]
    smem = pl.BlockSpec(memory_space=pltpu.SMEM)
    vmem = pl.BlockSpec(memory_space=pltpu.VMEM)
    bf16 = lambda *shape: jax.ShapeDtypeStruct(shape, jnp.bfloat16)
    ends = bf16(SUB + PLANES, halo, cols), bf16(SUB * (groups - 1), halo, cols)
    near, across, near_rest, across_rest = pl.pallas_call(
        functools.partial(pack_kernel, order),
        out_shape=(ends[0], ends[0], ends[1], ends[1]),
        in_specs=[pl.BlockSpec(memory_space=pltpu.HBM)] * 2,
        out_specs=[vmem] * 4,
        scratch_shapes=[
            pltpu.VMEM((2, halo, cols), jnp.float32),
            pltpu.SemaphoreType.DMA((2,)),
            pltpu.SemaphoreType.DMA((2 * waves * groups,)),
        ],
        compiler_params=pltpu.CompilerParams(vmem_limit_bytes=8 << 20),
        cost_estimate=pl.CostEstimate(flops=100000, bytes_accessed=2000000, transcendentals=0),
        name="pack",
    )(pltpu.with_memory_space_constraint(initial_fields, pltpu.HBM), pltpu.with_memory_space_constraint(conductivity, pltpu.HBM))
    across = lax.ppermute(across, "tile", between)
    near = lax.ppermute(near, "tile", beside)
    across_rest = lax.ppermute(across_rest, "tile", between)
    near_rest = lax.ppermute(near_rest, "tile", beside)
    tall = rows + 2 * halo
    width = cols // LANES
    high = (tall + 2) * SUB
    f32 = lambda *shape: jax.ShapeDtypeStruct(shape, jnp.float32)
    coefficients = pl.pallas_call(
        coefficients_kernel,
        out_shape=(
            f32(width, high, LANES), f32(width, high, LANES), f32(high, LANES),
            f32(waves, width, tall, LANES), f32(waves, width, tall, LANES), f32(high, LANES),
        ),
        in_specs=[smem, vmem, vmem, vmem],
        out_specs=[vmem] * 6,
        scratch_shapes=[
            pltpu.VMEM((width, tall + 2 * SUB, LANES), jnp.float32),
            pltpu.VMEM((waves, width, tall + SUB, LANES), jnp.float32),
        ],
        compiler_params=pltpu.CompilerParams(vmem_limit_bytes=16 << 20),
        cost_estimate=pl.CostEstimate(flops=4000000, bytes_accessed=6000000, transcendentals=0),
        name="coefficients",
    )(wavenumbers, near, conductivity, across)
    arrived = []
    for k, shift in enumerate(order):
        place = ((groups - 1) * pair, (k - 1) * pair) if k else (pair, 0)
        ends = (near_rest, across_rest) if k else (near, across)
        part = pl.pallas_call(
            functools.partial(sweep_kernel, shift, place),
            out_shape=f32(pair, rows, cols),
            in_specs=[smem] * 4 + [vmem] * 9,
            out_specs=vmem,
            scratch_shapes=[pltpu.VMEM((width, high, LANES), jnp.float32)] * 2
            + [pltpu.VMEM((high, LANES), jnp.float32)],
            compiler_params=pltpu.CompilerParams(vmem_limit_bytes=20 << 20),
            cost_estimate=pl.CostEstimate(flops=100000000, bytes_accessed=6000000, transcendentals=0),
        )(sweep_counts, quad_weights, electrode_cells, source_pairs, ends[0], initial_fields, ends[1], *coefficients)
        if shift:
            ring = [(i, (i + shift) % groups) for i in range(groups)]
            part = lax.ppermute(part, "wave", ring)
        arrived.append(part)
    return sum(arrived[1:], arrived[0])


def solution(mesh):
    placed = (P("wave", None, "tile", None), P("tile", None), P(), P(), P(), P(), P())
    return jax.shard_map(
        local, mesh=mesh, in_specs=placed, out_specs=P("wave", "tile", None), check_vma=False
    )
```

```python
import functools

import jax
import jax.numpy as jnp
from jax import lax
from jax.experimental import pallas as pl
from jax.experimental.pallas import tpu as pltpu
from jax.sharding import PartitionSpec as P


ITERS = 8
LOWER = 0.1
UPPER = 2.0
THETA = (UPPER + LOWER) / 2.0
DELTA = (UPPER - LOWER) / 2.0
SIGMA_ONE = THETA / DELTA
CURRENT = 2.0
DIAG = 2.0 * (THETA - 1.0) / DELTA
LANES = 128
SUB = 8
UNROLL = 4
BATCH = 8
PLANES = 3


def chebyshev_table():
    values = [1.0, SIGMA_ONE]
    for _ in range(ITERS):
        values.append(2.0 * SIGMA_ONE * values[-1] - values[-2])
    return values


TABLE = chebyshev_table()


def pick(values, t):
    result = jnp.float32(values[0])
    for k in range(1, len(values)):
        result = jnp.where(t == k, jnp.float32(values[k]), result)
    return result


def exchange(values, lanes):
    values = list(values)
    step = len(values) // 2
    while step:
        upper = lax.rem(lax.div(lanes, step), 2) == 1
        for i in range(len(values)):
            if i & step:
                continue
            low, high = values[i], values[i + step]
            values[i] = jnp.where(upper, pltpu.roll(high, step, 1), low)
            values[i + step] = jnp.where(upper, high, pltpu.roll(low, LANES - step, 1))
        step //= 2
    return values


def wrap_west(value, lanes, span):
    return jnp.take_along_axis(
        value, jnp.where(lanes < span, lanes + (LANES - span - 1), lanes - span), axis=1,
        mode="promise_in_bounds",
    )


def wrap_east(value, lanes, span):
    return jnp.take_along_axis(
        value, jnp.where(lanes < LANES - span, lanes + span, lanes - (LANES - span - 1)), axis=1,
        mode="promise_in_bounds",
    )


def pieces(value):
    return [value[:, j:j + LANES] for j in range(0, value.shape[1], LANES)]


def coefficients_kernel(
    wavenumbers, near, cond, across,
    c_north, c_east, c_wrap, root, inverse, q_first, cond_pad, q_pad,
):
    rows, _ = cond.shape
    halo = near.shape[1]
    waves, width = root.shape[:2]
    tall = rows + 2 * halo
    pair = SUB // waves
    first = lax.axis_index("wave") * waves
    lanes = lax.broadcasted_iota(jnp.int32, (SUB, LANES), 1)
    squares = [wavenumbers[first + w] * wavenumbers[first + w] for w in range(waves)]
    blank = jnp.zeros((SUB, LANES), jnp.float32)

    def store(at, value):
        for j, part in enumerate(exchange(pieces(value), lanes)):
            cond_pad[j, pl.ds(at, SUB), :] = part

    for j in range(width):
        cond_pad[j, pl.ds(0, SUB), :] = blank
        cond_pad[j, pl.ds(SUB + tall, SUB), :] = blank
        for w in range(waves):
            q_pad[w, j, pl.ds(0, SUB), :] = blank
    low = lax.rem(lax.axis_index("tile"), 2) == 0
    for ref, at in (
        (near, jnp.where(low, SUB + halo + rows, SUB)),
        (across, jnp.where(low, SUB, SUB + halo + rows)),
    ):
        planes = [ref[SUB + i].astype(jnp.float32) for i in range(PLANES)]
        store(pl.multiple_of(at, SUB), functools.reduce(jnp.add, planes))

    for k in range(rows // SUB):
        store(SUB + halo + k * SUB, cond[pl.ds(k * SUB, SUB), :])

    def tile(k, carry):
        base = pl.multiple_of(k * SUB, SUB)
        plain = pl.ds(base, SUB)
        mid = [cond_pad[j, pl.ds(base + SUB, SUB), :] for j in range(width)]
        north, east, diagonal = [], [], []
        for j in range(width):
            up = cond_pad[j, pl.ds(base + SUB - 1, SUB), :]
            down = cond_pad[j, pl.ds(base + SUB + 1, SUB), :]
            if j + 1 < width:
                right = mid[j + 1]
            else:
                right = jnp.where(lanes == LANES - 1, 0.0, wrap_east(mid[0], lanes, width))
            left = mid[j - 1] if j else jnp.where(lanes == 0, 0.0, wrap_west(mid[-1], lanes, width))
            north.append(0.5 * (mid[j] + up))
            east.append(0.5 * (mid[j] + right))
            diagonal.append(north[j] + 0.5 * (mid[j] + down) + 0.5 * (mid[j] + left) + east[j])
        east[-1] = jnp.where(lanes == LANES - 1, 0.0, east[-1])
        for w in range(waves):
            q = []
            for j in range(width):
                full = diagonal[j] + squares[w] * mid[j]
                q.append(jnp.where(mid[j] > 0.0, lax.rsqrt(full), 0.0))
                root[w, j, plain, :] = full * q[j]
                inverse[w, j, plain, :] = q[j]
                q_pad[w, j, pl.ds(base + SUB, SUB), :] = q[j]
            for j in range(width):
                right = q[j + 1] if j + 1 < width else wrap_east(q[0], lanes, width)
                scaled = (2.0 / DELTA) * q[j]
                north_w = scaled * q_pad[w, j, pl.ds(base + SUB - 1, SUB), :] * north[j]
                east_w = scaled * right * east[j]
                for s in range(pair):
                    spot = pl.ds((base + 1) * SUB + w * pair + s, SUB, stride=SUB)
                    c_north[j, spot, :] = north_w
                    c_east[j, spot, :] = east_w
                    if j == 0:
                        q_first[spot, :] = jnp.where(lanes == 0, q[0], 0.0)
                    if j == width - 1:
                        c_wrap[spot, :] = jnp.where(lanes == 0, 0.0, wrap_west(east_w, lanes, width))
        return carry

    lax.fori_loop(0, tall // SUB, tile, 0)


def pack_kernel(order, fields, cond, near, across, near_rest, across_rest, edge, edge_sems, sems):
    waves, sources, rows, _ = fields.shape
    groups = len(order)
    pair = sources // groups
    halo = near.shape[1]
    wave_pos = lax.axis_index("wave")
    low = lax.rem(lax.axis_index("tile"), 2) == 0
    ends = jnp.where(low, rows - halo, 0), jnp.where(low, 0, rows - halo)
    edges = [
        pltpu.make_async_copy(
            cond.at[pl.ds(pl.multiple_of(end, halo), halo), :], edge.at[i], edge_sems.at[i]
        )
        for i, end in enumerate(ends)
    ]
    for copy in edges:
        copy.start()
    copies = []
    for k, shift in enumerate(order):
        chunk = lax.rem(wave_pos + shift, groups)
        for (first, rest), end in zip(((across, across_rest), (near, near_rest)), ends[::-1]):
            for w in range(waves):
                source = fields.at[
                    w, pl.ds(chunk * pair, pair), pl.ds(pl.multiple_of(end, halo), halo), :
                ]
                if k == 0:
                    target = first.at[pl.ds(w * pair, pair)]
                else:
                    target = rest.at[pl.ds((w * (groups - 1) + k - 1) * pair, pair)]
                copies.append(pltpu.make_async_copy(source, target, sems.at[len(copies)]))
    for copy in copies:
        copy.start()
    for k, ref in enumerate((near, across)):
        edges[k].wait()
        value = edge[k]
        for i in range(PLANES):
            part = value.astype(jnp.bfloat16)
            ref[SUB + i] = part
            value = value - part.astype(jnp.float32)
    for copy in copies:
        copy.wait()


def sweep_kernel(
    shift, place, counts, weights, cells, pairs,
    near, own, across, c_north, c_east, c_wrap, root, inverse, q_first,
    out, u_even, u_odd, inject,
):
    waves, sources, rows, cols = own.shape
    halo = near.shape[1]
    pair = out.shape[0]
    per, skip = place
    tall = rows + 2 * halo
    width = cols // LANES
    wave_pos = lax.axis_index("wave")
    first_row = lax.axis_index("tile") * rows
    first_wave = wave_pos * waves
    chunk = lax.rem(wave_pos + shift, sources // pair)
    count = [counts[first_wave + w] for w in range(waves)]
    limit = functools.reduce(jnp.maximum, count)
    least = functools.reduce(jnp.minimum, count)
    ids = lax.broadcasted_iota(jnp.int32, (SUB, LANES), 0)
    lanes = lax.broadcasted_iota(jnp.int32, (SUB, LANES), 1)
    count_of = functools.reduce(
        lambda v, w: jnp.where(lax.div(ids, pair) == w, count[w], v), range(waves), jnp.zeros_like(ids)
    )

    def spot_of(r):
        return pl.ds(pl.multiple_of(r * SUB, SUB), SUB)

    wide = lax.broadcasted_iota(jnp.int32, (2 * SUB, LANES), 1)

    def begin_tile(bases, load):
        for w in range(waves):
            for s in range(pair):
                for j, part in enumerate(exchange(pieces(load(w, s)), wide)):
                    part = part.astype(jnp.float32)
                    for half, base in enumerate(bases):
                        spot = pl.ds((base + 1) * SUB + w * pair + s, SUB, stride=SUB)
                        u_even[j, spot, :] = (
                            part[half * SUB:(half + 1) * SUB] * root[w, j, pl.ds(base, SUB), :]
                        )

    def begin_own(k, carry):
        at = pl.multiple_of(k * 2 * SUB, 2 * SUB)
        base = pl.multiple_of(halo + at, SUB)
        begin_tile((base, base + SUB), lambda w, s: own[w, chunk * pair + s, pl.ds(at, 2 * SUB), :])
        return carry

    lax.fori_loop(0, rows // (2 * SUB), begin_own, 0)
    low = lax.rem(lax.axis_index("tile"), 2) == 0
    begin_tile(
        (
            pl.multiple_of(jnp.where(low, halo + rows, 0), SUB),
            pl.multiple_of(jnp.where(low, 0, halo + rows), SUB),
        ),
        lambda w, s: jnp.concatenate([ref[w * per + skip + s] for ref in (near, across)], axis=0),
    )

    inject[...] = jnp.zeros(inject.shape, jnp.float32)
    for s in range(pair):
        for pole, sign in ((0, 1.0), (1, -1.0)):
            r = cells[pairs[chunk * pair + s, pole]] - first_row + halo

            @pl.when(jnp.logical_and(r >= 0, r < tall))
            def _():
                here = spot_of(r + 1)
                add = jnp.where(lax.rem(ids, pair) == s, q_first[here, :], 0.0)
                inject[here, :] = inject[here, :] + sign * add

    def level(t, src, dst, first):
        depth = lax.div(limit - t + 3, 4) * 4
        begin = halo - depth + 1
        boost = pick([0.0, CURRENT / DELTA] + [2.0 * CURRENT / DELTA * v for v in TABLE[1:ITERS]], t)
        live = count_of >= t

        def wraps(r, size):
            spots = [spot_of(r + i) for i in range(size)]
            return (
                [wrap_west(src[width - 1, spot, :], lanes, width) for spot in spots]
                + [wrap_east(src[0, spot, :], lanes, width) for spot in spots]
            )

        def group(r, size, masked, turned):
            spots = [spot_of(r + i - 1) for i in range(size + 2)]
            inner = range(1, size + 1)
            load = lambda ref, j, many: {i: ref[j, spots[i], :] for i in many}
            around = range(size + 2)
            past = {i: c_wrap[spots[i], :] * turned[i - 1] for i in inner}
            mid = load(src, 0, around)
            for j in range(width):
                if j + 1 < width:
                    after = load(src, j + 1, around)
                else:
                    after = {i: turned[size + i - 1] for i in inner}
                north = load(c_north, j, range(1, size + 2))
                east = load(c_east, j, inner)
                before = past
                past = {i: east[i] * mid[i] for i in inner}
                for i in inner:
                    total = (
                        (north[i] * mid[i - 1] + north[i + 1] * mid[i + 1])
                        + (east[i] * after[i] + before[i])
                    )
                    if first:
                        total = 0.5 * (total + DIAG * mid[i])
                    else:
                        total = total + (DIAG * mid[i] - dst[j, spots[i], :])
                    if j == 0:
                        total = total + boost * inject[spots[i], :]
                    if masked:
                        total = jnp.where(live, total, mid[i])
                    dst[j, spots[i], :] = total
                mid = after

        def loop(masked):
            def body(k, carry):
                r = begin + BATCH * k
                turned = wraps(r, BATCH)
                for i in range(0, BATCH, UNROLL):
                    group(
                        r + i, UNROLL, masked,
                        turned[i:i + UNROLL] + turned[BATCH + i:BATCH + i + UNROLL],
                    )
                return carry

            lax.fori_loop(0, (rows + 2 * depth) // BATCH, body, 0)

        if first:
            loop(False)
        else:
            pl.when(t <= least)(lambda: loop(False))
            pl.when(t > least)(lambda: loop(True))

    level(1, u_even, u_odd, True)

    def two(k, carry):
        level(2 * k, u_odd, u_even, False)
        pl.when(2 * k + 1 <= limit)(lambda: level(2 * k + 1, u_even, u_odd, False))
        return carry

    lax.fori_loop(1, lax.div(limit, 2) + 1, two, 0)
    ends = [0.0] + [1.0 / v for v in TABLE[1:ITERS + 1]]
    gains = [weights[first_wave + w] * pick(ends, count[w]) for w in range(waves)]

    def finish(last):
        def body(k, carry):
            at = pl.multiple_of(k * SUB, SUB)
            base = at + halo
            for s in range(pair):
                sums = []
                for j in range(width):
                    terms = [
                        (gains[w] * inverse[w, j, pl.ds(base, SUB), :])
                        * last[j, pl.ds((base + 1) * SUB + w * pair + s, SUB, stride=SUB), :]
                        for w in range(waves)
                    ]
                    sums.append(functools.reduce(jnp.add, terms))
                for j, part in enumerate(sums):
                    out[s, pl.ds(at, SUB), pl.ds(j * LANES, LANES)] = part
            return carry

        lax.fori_loop(0, rows // SUB, body, 0)

    pl.when(lax.rem(limit, 2) == 0)(lambda: finish(u_even))
    pl.when(lax.rem(limit, 2) == 1)(lambda: finish(u_odd))
    for s in range(pair):
        for k in range(rows // SUB):
            cuts = [(s, pl.ds(k * SUB, SUB), pl.ds(j * LANES, LANES)) for j in range(width)]
            for cut, part in zip(cuts, exchange([out[cut] for cut in cuts], lanes)):
                out[cut] = part


def local(
    initial_fields, conductivity, wavenumbers, quad_weights, sweep_counts, electrode_cells,
    source_pairs,
):
    rows, cols = conductivity.shape
    waves, sources = initial_fields.shape[:2]
    halo = ITERS
    groups = lax.axis_size("wave")
    pair = sources // groups
    count = lax.axis_size("tile")
    order = [groups // 2] + [j for j in range(1, groups) if j != groups // 2] + [0]
    beside = [(i, i ^ 1) for i in range(count)]
    between = [(i, i + 1 if i % 2 else i - 1) for i in range(1, count - 1)]
    smem = pl.BlockSpec(memory_space=pltpu.SMEM)
    vmem = pl.BlockSpec(memory_space=pltpu.VMEM)
    bf16 = lambda *shape: jax.ShapeDtypeStruct(shape, jnp.bfloat16)
    ends = bf16(SUB + PLANES, halo, cols), bf16(SUB * (groups - 1), halo, cols)
    near, across, near_rest, across_rest = pl.pallas_call(
        functools.partial(pack_kernel, order),
        out_shape=(ends[0], ends[0], ends[1], ends[1]),
        in_specs=[pl.BlockSpec(memory_space=pltpu.HBM)] * 2,
        out_specs=[vmem] * 4,
        scratch_shapes=[
            pltpu.VMEM((2, halo, cols), jnp.float32),
            pltpu.SemaphoreType.DMA((2,)),
            pltpu.SemaphoreType.DMA((2 * waves * groups,)),
        ],
        compiler_params=pltpu.CompilerParams(vmem_limit_bytes=8 << 20),
        cost_estimate=pl.CostEstimate(flops=100000, bytes_accessed=2000000, transcendentals=0),
        name="pack",
    )(pltpu.with_memory_space_constraint(initial_fields, pltpu.HBM), pltpu.with_memory_space_constraint(conductivity, pltpu.HBM))
    across = lax.ppermute(across, "tile", between)
    near = lax.ppermute(near, "tile", beside)
    across_rest = lax.ppermute(across_rest, "tile", between)
    near_rest = lax.ppermute(near_rest, "tile", beside)
    tall = rows + 2 * halo
    width = cols // LANES
    high = (tall + 2) * SUB
    f32 = lambda *shape: jax.ShapeDtypeStruct(shape, jnp.float32)
    coefficients = pl.pallas_call(
        coefficients_kernel,
        out_shape=(
            f32(width, high, LANES), f32(width, high, LANES), f32(high, LANES),
            f32(waves, width, tall, LANES), f32(waves, width, tall, LANES), f32(high, LANES),
        ),
        in_specs=[smem, vmem, vmem, vmem],
        out_specs=[vmem] * 6,
        scratch_shapes=[
            pltpu.VMEM((width, tall + 2 * SUB, LANES), jnp.float32),
            pltpu.VMEM((waves, width, tall + SUB, LANES), jnp.float32),
        ],
        compiler_params=pltpu.CompilerParams(vmem_limit_bytes=16 << 20),
        cost_estimate=pl.CostEstimate(flops=4000000, bytes_accessed=6000000, transcendentals=0),
        name="coefficients",
    )(wavenumbers, near, conductivity, across)
    arrived = []
    for k, shift in enumerate(order):
        place = ((groups - 1) * pair, (k - 1) * pair) if k else (pair, 0)
        ends = (near_rest, across_rest) if k else (near, across)
        part = pl.pallas_call(
            functools.partial(sweep_kernel, shift, place),
            out_shape=f32(pair, rows, cols),
            in_specs=[smem] * 4 + [vmem] * 9,
            out_specs=vmem,
            scratch_shapes=[pltpu.VMEM((width, high, LANES), jnp.float32)] * 2
            + [pltpu.VMEM((high, LANES), jnp.float32)],
            compiler_params=pltpu.CompilerParams(vmem_limit_bytes=20 << 20),
            cost_estimate=pl.CostEstimate(flops=100000000, bytes_accessed=6000000, transcendentals=0),
        )(sweep_counts, quad_weights, electrode_cells, source_pairs, ends[0], initial_fields, ends[1], *coefficients)
        if shift:
            ring = [(i, (i + shift) % groups) for i in range(groups)]
            part = lax.ppermute(part, "wave", ring)
        arrived.append(part)
    return sum(arrived[1:], arrived[0])


def solution(mesh):
    placed = (P("wave", None, "tile", None), P("tile", None), P(), P(), P(), P(), P())
    return jax.shard_map(
        local, mesh=mesh, in_specs=placed, out_specs=P("wave", "tile", None), check_vma=False
    )
```
